32 devices in a mesh: prow: 4 (over y, x), pcol: 8 (over z, core).
Axes of the slice: x: 2, y: 2, z: 4, core: 2. Of those that a mesh axis runs over, the one named last changes fastest.
Arguments:
- diag_block: float32 [128, 128], replicated, may hold values from 0 to 1.03, as said below
- panel: float32 [8192, 128], P(('prow', 'pcol')), may hold values from -0.2 to 1.2
- slab: float32 [8192, 2048], P('prow', 'pcol'), may hold values from -6 to 6
Outputs:
- slab_next: float32 [8192, 2048], P('prow', 'pcol')
- panel_factor: float32 [8192, 128], P(('prow', 'pcol'))
The draws below stay inside these ranges and needn't reach their ends.
Inputs may be any that keep to these rules, and one draw needn't show every extreme that they name: diag_block is symmetric positive definite.
All inputs are finite; a program needn't handle non-finite values.
Results may differ from the reference program's by a relative error of at most 0.00091.
Values may be sent and summed in bfloat16 or wider, within the bound.
No kernel may reach another device: no remote copies, remote signals or barrier semaphores. Data moves between devices by JAX's collectives and lax.ppermute only.
A program may use at most 64 MiB of HBM per device.

```python
import math
import jax
import jax.numpy as jnp
import numpy as np
from jax import lax

NB = 128
ROWS_DEV = 2048
COLS_DEV = 256
ROWS = 8192
COLS = 2048
N_PROW = 4
N_PCOL = 8


def site_points(key, count):
    side = math.sqrt(NB)
    coord_key, other_key = jax.random.split(key)
    first = jax.random.uniform(coord_key, (count,), jnp.float32, 0.0, side)
    second = jax.random.uniform(other_key, (count,), jnp.float32, 0.0, side)
    return (first, second)


def kernel_values(first_a, second_a, first_b, second_b, length_scale):
    gap_one = first_a[:, None] - first_b[None, :]
    gap_two = second_a[:, None] - second_b[None, :]
    distance = jnp.sqrt(gap_one * gap_one + gap_two * gap_two)
    return jnp.exp(-distance / length_scale)


def draw_diag_block(key, part):
    length_scale = 1.5
    first, second = site_points(jax.random.fold_in(key, 11), NB)
    covariance = kernel_values(first, second, first, second, length_scale)
    return covariance + 0.03 * jnp.eye(NB, dtype=jnp.float32)


def draw_panel(key, part):
    length_scale = 1.5
    first, second = site_points(jax.random.fold_in(key, 11), NB)
    far_first, far_second = site_points(jax.random.fold_in(key, 12), ROWS)
    cross = kernel_values(far_first, far_second, first, second, length_scale)
    noise_key = jax.random.fold_in(key, 13)
    noise = 0.05 * jax.random.truncated_normal(noise_key, -4.0, 4.0, (ROWS, NB), jnp.float32)
    return cross + noise


def levels(own_key, shape, cuts, least, largest):
    gain = 1.0
    for dim, blocks in cuts:
        heights = jax.random.uniform(jax.random.fold_in(jax.random.fold_in(own_key, 6), dim), (blocks,), jnp.float32, least / len(cuts), largest / len(cuts))
        gain = gain * jnp.repeat(jnp.exp(heights), shape[dim] // blocks).reshape((-1,) + (1,) * (len(shape) - 1 - dim))
    return gain


def normal_values(stream_key, extent, deviation, reach, cuts=(), kind=jnp.bfloat16):
    gain = levels(stream_key, extent, cuts, -0.22, 0.18) if cuts else 1.0
    entries = jax.random.normal(stream_key, extent, jnp.float32) * deviation * gain
    return jnp.minimum(jnp.maximum(entries, -reach), reach).astype(kind)


def setup_inputs(seed: int = 0) -> dict:
    key_list = jax.random.split(jax.random.key(seed), 4)
    diag_block = draw_diag_block(jax.random.fold_in(key_list[3], 71), 0)
    panel = draw_panel(jax.random.fold_in(key_list[3], 71), 0)
    slab = normal_values(key_list[2], (ROWS, COLS), 1.0, 6.0, ((0, 4), (1, 8)), jnp.float32)
    return {"diag_block": diag_block, "panel": panel, "slab": slab}


def reference(diag_block, panel, slab):
    factor_block = jnp.linalg.cholesky(diag_block)
    panel_factor = lax.linalg.triangular_solve(factor_block, panel, left_side=False, lower=True, transpose_a=True)
    low_panel = panel_factor.astype(jnp.bfloat16)
    local_blocks = ROWS_DEV // NB
    column_blocks = COLS_DEV // NB
    stored_list = []
    for column_block in range(N_PCOL * column_blocks):
        owner_column = column_block // column_blocks
        position = column_block % column_blocks
        matrix_block = owner_column + N_PCOL * position
        stored_list.append(matrix_block % N_PROW * local_blocks + matrix_block // N_PROW)
    row_index = (np.array(stored_list, dtype=np.int32)[:, None] * NB + np.arange(NB, dtype=np.int32)[None, :]).reshape(-1)
    column_panel = low_panel[row_index]
    product = jnp.dot(low_panel.astype(jnp.float32), column_panel.T.astype(jnp.float32), preferred_element_type=jnp.float32)
    slab_next = slab - product
    return (slab_next, panel_factor)
```

```python
import jax
import jax.numpy as jnp
from jax import lax
from jax.experimental import pallas as pl
from jax.experimental.pallas import tpu as pltpu
from jax.sharding import PartitionSpec as P

GROUP = 8
EXACT = lax.Precision.HIGHEST
NT = (((1,), (1,)), ((), ()))


def inverse_factor_kernel(diag_ref, out_ref):
    n = diag_ref.shape[0]
    lane = lax.broadcasted_iota(jnp.int32, (GROUP, n), 1)
    sub = lax.broadcasted_iota(jnp.int32, (GROUP, n), 0)
    rows = [diag_ref[i : i + GROUP, :] for i in range(0, n, GROUP)]

    def column(x, at):
        return jnp.broadcast_to(x[:, at : at + 1], (GROUP, n))

    def row(x, at):
        return jnp.broadcast_to(x[at : at + 1, :], (GROUP, n))

    for b in range(n // GROUP):
        first = b * GROUP
        inside = (lane >= first) & (lane < first + GROUP)
        cols = [column(rows[b], first + j) for j in range(GROUP)]
        work = jnp.where(inside, jnp.where(lane - first == sub, 1.0, 0.0), rows[b])
        scale, scaled, cross = [], [], {}
        for k in range(GROUP):
            scale.append(lax.rsqrt(row(cols[k], k)))
            scaled.append(row(work, k) * scale[k])
            if k < GROUP - 1:
                factor = jnp.where(sub > k, cols[k] * scale[k], 0.0)
                for j in range(k + 1, GROUP):
                    cross[k, j] = row(cols[j], k) * scale[k]
                    cols[j] = cols[j] - factor * cross[k, j]
                work = work - factor * scaled[k]
        done = scaled[0]
        for k in range(1, GROUP):
            done = jnp.where(sub == k, scaled[k], done)
        out_ref[first : first + GROUP, :] = jnp.where(lane <= sub + first, done, 0.0)
        for i in range(b + 1, n // GROUP):
            cols = [column(rows[i], first + j) for j in range(GROUP)]
            rest = jnp.where(inside, 0.0, rows[i])
            for k in range(GROUP):
                factor = cols[k] * scale[k]
                for j in range(k + 1, GROUP):
                    cols[j] = cols[j] - factor * cross[k, j]
                rest = rest - factor * scaled[k]
            rows[i] = rest


def inverse_factor(diag_block):
    n = diag_block.shape[0]
    return pl.pallas_call(
        inverse_factor_kernel,
        out_shape=jax.ShapeDtypeStruct((n, n), jnp.float32),
        in_specs=[pl.BlockSpec(memory_space=pltpu.VMEM)],
        out_specs=pl.BlockSpec(memory_space=pltpu.VMEM),
        cost_estimate=pl.CostEstimate(flops=20_000_000, bytes_accessed=8 * n * n, transcendentals=n),
        name="inverse_factor",
    )(diag_block)


def solve(rows, inverse):
    return lax.dot_general(rows, inverse, NT, precision=EXACT, preferred_element_type=jnp.float32)


def update_kernel(pieces, parts, inverse_ref, *refs):
    piece_refs, refs = refs[:pieces], refs[pieces:]
    part_refs, refs = refs[:parts], refs[parts:]
    slab_ref, next_ref, factor_ref, out_vmem, sems = refs
    me = lax.axis_index("pcol")
    height = piece_refs[0].shape[0]
    inverse = inverse_ref[...]
    column = part_refs[0][...]
    for ref in part_refs[1:]:
        column = column + ref[...]
    column = solve(column, inverse).astype(jnp.bfloat16)
    copies = []
    for k in range(pieces):
        at = pl.ds(pl.multiple_of((me ^ k) * height, height), height)
        solved = solve(piece_refs[k][...], inverse)
        if k == 0:
            factor_ref[...] = solved
        product = lax.dot_general(solved.astype(jnp.bfloat16), column, NT, preferred_element_type=jnp.float32)
        out_vmem[at, :] = slab_ref[at, :] - product
        copy = pltpu.make_async_copy(out_vmem.at[at, :], next_ref.at[at, :], sems.at[k])
        copy.start()
        copies.append(copy)
    for copy in copies:
        copy.wait()


def update(inverse, pieces, parts, slab):
    import functools

    vmem = pl.BlockSpec(memory_space=pltpu.VMEM)
    return pl.pallas_call(
        functools.partial(update_kernel, len(pieces), len(parts)),
        out_shape=(
            jax.ShapeDtypeStruct(slab.shape, jnp.float32),
            jax.ShapeDtypeStruct(pieces[0].shape, jnp.float32),
        ),
        in_specs=[vmem] * (len(pieces) + len(parts) + 2),
        out_specs=(pl.BlockSpec(memory_space=pl.ANY), vmem),
        scratch_shapes=[
            pltpu.VMEM(slab.shape, jnp.float32),
            pltpu.SemaphoreType.DMA((len(pieces),)),
        ],
        cost_estimate=pl.CostEstimate(flops=1_000_000_000, bytes_accessed=12 * slab.size, transcendentals=0),
        name="update",
    )(inverse, *pieces, *parts, slab)


def per_device(diag_block, panel, slab):
    prows = lax.axis_size("prow")
    pcols = lax.axis_size("pcol")
    width = diag_block.shape[0]
    spread = pcols // prows
    here = slab.shape[1] // width
    me = lax.axis_index("pcol")
    height = panel.shape[0]

    def flip(x, k):
        return lax.ppermute(x, "pcol", [(i, i ^ k) for i in range(pcols)])

    pieces = [None] * pcols
    pieces[0] = panel
    order = sorted(range(2, pcols, 2), key=lambda k: (k != 4, k != 6, k))
    for k in order:
        pieces[k] = flip(panel, k)
    inverse = inverse_factor(diag_block)
    for k in range(0, pcols, 2):
        pieces[k + 1] = flip(pieces[k], 1)

    stacked = jnp.stack(pieces)
    shards = []
    blocks = []
    for position in range(here):
        block = me // prows + position * spread
        strips = []
        step = min(width, height)
        for offset in range(0, width, step):
            row_at = block * width + offset
            shard = row_at // height
            strips.append(
                lax.dynamic_slice(stacked, (shard ^ me, row_at % height, 0), (1, step, width))[0]
            )
        blocks.extend(strips)
    wanted = jnp.concatenate(blocks, 0)
    root_of = [q % prows for q in range(pcols)]
    parts = [jnp.where(lax.axis_index("prow") == me % prows, wanted, 0.0)]
    for k in range(1, prows):
        pairs = [(root_of[q] * pcols + q, (root_of[q] ^ k) * pcols + q) for q in range(pcols)]
        parts.append(lax.ppermute(wanted, ("prow", "pcol"), pairs))
    slab_next, solved = update(inverse, pieces, parts, slab)
    return slab_next, solved


def solution(mesh):
    placed = (P(), P(("prow", "pcol"), None), P("prow", "pcol"))
    return jax.shard_map(
        per_device,
        mesh=mesh,
        in_specs=placed,
        out_specs=(P("prow", "pcol"), P(("prow", "pcol"), None)),
        check_vma=False,
    )
```

```python
import functools

import jax
import jax.numpy as jnp
from jax import lax
from jax.experimental import pallas as pl
from jax.experimental.pallas import tpu as pltpu
from jax.sharding import PartitionSpec as P


GROUP = 8
EXACT = lax.Precision.HIGHEST
NT = (((1,), (1,)), ((), ()))


def inverse_factor_kernel(diag_ref, out_ref):
    n = diag_ref.shape[0]
    lane = lax.broadcasted_iota(jnp.int32, (GROUP, n), 1)
    sub = lax.broadcasted_iota(jnp.int32, (GROUP, n), 0)
    rows = [diag_ref[i : i + GROUP, :] for i in range(0, n, GROUP)]

    def column(x, at):
        return jnp.broadcast_to(x[:, at : at + 1], (GROUP, n))

    def row(x, at):
        return jnp.broadcast_to(x[at : at + 1, :], (GROUP, n))

    for b in range(n // GROUP):
        first = b * GROUP
        inside = (lane >= first) & (lane < first + GROUP)
        cols = [column(rows[b], first + j) for j in range(GROUP)]
        work = jnp.where(inside, jnp.where(lane - first == sub, 1.0, 0.0), rows[b])
        scale, scaled, cross = [], [], {}
        for k in range(GROUP):
            scale.append(lax.rsqrt(row(cols[k], k)))
            scaled.append(row(work, k) * scale[k])
            if k < GROUP - 1:
                factor = jnp.where(sub > k, cols[k] * scale[k], 0.0)
                for j in range(k + 1, GROUP):
                    cross[k, j] = row(cols[j], k) * scale[k]
                    cols[j] = cols[j] - factor * cross[k, j]
                work = work - factor * scaled[k]
        done = scaled[0]
        for k in range(1, GROUP):
            done = jnp.where(sub == k, scaled[k], done)
        out_ref[first : first + GROUP, :] = jnp.where(lane <= sub + first, done, 0.0)
        for i in range(b + 1, n // GROUP):
            cols = [column(rows[i], first + j) for j in range(GROUP)]
            rest = jnp.where(inside, 0.0, rows[i])
            for k in range(GROUP):
                factor = cols[k] * scale[k]
                for j in range(k + 1, GROUP):
                    cols[j] = cols[j] - factor * cross[k, j]
                rest = rest - factor * scaled[k]
            rows[i] = rest


def inverse_factor(diag_block):
    n = diag_block.shape[0]
    return pl.pallas_call(
        inverse_factor_kernel,
        out_shape=jax.ShapeDtypeStruct((n, n), jnp.float32),
        in_specs=[pl.BlockSpec(memory_space=pltpu.VMEM)],
        out_specs=pl.BlockSpec(memory_space=pltpu.VMEM),
        cost_estimate=pl.CostEstimate(flops=2_000_000_000, bytes_accessed=8 * n * n, transcendentals=n),
        compiler_params=pltpu.CompilerParams(vmem_limit_bytes=2 << 20),
        name="inverse_factor",
    )(diag_block)


class Plan:
    def __init__(self, prows, pcols, width, height, here):
        self.prows, self.pcols, self.height = prows, pcols, height
        self.step = min(width, height)
        spread = pcols // prows

        def strips(column):
            found = []
            for position in range(here):
                block = column // prows + position * spread
                for offset in range(0, width, self.step):
                    at = block * width + offset
                    found.append((at // height, at % height))
            return found

        self.total = here * width
        parity = [shard % 2 for shard, _ in strips(0)]
        assert parity == [s % 2 for s in range(len(parity))]
        self.strips_each = len(parity) // 2
        self.flips = []
        for row in range(prows):
            first = []
            for column in range(row, pcols, prows):
                for shard, _ in strips(column):
                    k = 2 * ((shard // 2) ^ (column // 2))
                    if k and k not in first:
                        first.append(k)
            first.sort(reverse=row < prows // 2 and False)
            first.sort(key=lambda k: (k != 4, -k))
            rest = [k for k in range(pcols - 2, 0, -2) if k not in first]
            self.flips.append([0] + first + rest)
        self.slots = pcols // 2
        self.starts = []
        last = 0
        for row in range(prows):
            for me in range(pcols):
                mine = [0] * self.strips_each
                for column in (me, me ^ 1):
                    if column % prows == row:
                        own = [s for s in strips(column) if s[0] % 2 == me % 2]
                        slot = [self.flips[row].index(2 * ((s // 2) ^ (me // 2))) for s, _ in own]
                        last = max(last, *slot)
                        mine = [j * height + at for j, (_, at) in zip(slot, own)]
                self.starts.append(mine)
        self.early = last + 1

    def pairs(self, slot):
        return [
            (row * self.pcols + i, row * self.pcols + (i ^ self.flips[row][slot]))
            for row in range(self.prows)
            for i in range(self.pcols)
        ]

    def pass_on(self, k):
        return [
            (row * self.pcols + i, (row ^ k) * self.pcols + i)
            for row in range(self.prows)
            for i in range(self.pcols)
            if row in (i % self.prows, (i ^ 1) % self.prows)
        ]


def pick(values, index):
    chosen = jnp.int32(values[0])
    for i, value in enumerate(values[1:], 1):
        chosen = jnp.where(index == i, jnp.int32(value), chosen)
    return chosen


def solve(rows, inverse):
    return lax.dot_general(rows, inverse, NT, precision=EXACT, preferred_element_type=jnp.float32)


def solve_kernel(plan, count, own, inverse_ref, *refs):
    piece_refs, refs = refs[:count], refs[count:]
    inverse = inverse_ref[...]
    for j, ref in enumerate(piece_refs):
        solved = solve(ref[...], inverse)
        if own and j == 0:
            refs[2][...] = solved
        refs[0][j * plan.height : (j + 1) * plan.height, :] = solved.astype(jnp.bfloat16)
    if own:
        device = lax.axis_index("prow") * plan.pcols + lax.axis_index("pcol")
        for s in range(plan.strips_each):
            start = pl.multiple_of(pick([v[s] for v in plan.starts], device), plan.step)
            refs[1][s * plan.step : (s + 1) * plan.step, :] = refs[0][pl.ds(start, plan.step), :]


def solve_pieces(plan, inverse, pieces, own):
    width = inverse.shape[0]
    count = len(pieces)
    vmem = pl.BlockSpec(memory_space=pltpu.VMEM)
    outs = [jax.ShapeDtypeStruct((count * plan.height, width), jnp.bfloat16)]
    if own:
        outs.append(jax.ShapeDtypeStruct((plan.strips_each * plan.step, width), jnp.bfloat16))
        outs.append(jax.ShapeDtypeStruct((plan.height, width), jnp.float32))
    return pl.pallas_call(
        functools.partial(solve_kernel, plan, count, own),
        out_shape=tuple(outs),
        in_specs=[vmem] * (count + 1),
        out_specs=tuple([vmem] * len(outs)),
        cost_estimate=pl.CostEstimate(
            flops=12 * count * plan.height * width * width, bytes_accessed=6 * count * plan.height * width, transcendentals=0
        ),
        compiler_params=pltpu.CompilerParams(vmem_limit_bytes=4 << 20),
        name="solve_own" if own else "solve_rest",
    )(inverse, *pieces)


def update_kernel(plan, groups, x_refs_n, *refs):
    x_refs, refs = refs[:x_refs_n], refs[x_refs_n:]
    mine_ref, other_ref, slab_ref, next_ref, column, out_vmem, sems = refs
    row, me = lax.axis_index("prow"), lax.axis_index("pcol")
    parity = lax.rem(me, 2)
    step = plan.step
    for s in range(plan.strips_each):
        for ref, side in ((mine_ref, parity), (other_ref, 1 - parity)):
            at = pl.multiple_of((2 * s + side) * step, step)
            column[pl.ds(at, step), :] = ref[s * step : (s + 1) * step, :]
    whole = column[...]
    flips = [pick([f[j] for f in plan.flips], row) for j in range(plan.slots)]
    copies = []
    for ref, (slots, side) in zip(x_refs, groups):
        for n, j in enumerate(slots):
            at = pl.ds(pl.multiple_of((me ^ side ^ flips[j]) * plan.height, plan.height), plan.height)
            product = lax.dot_general(
                ref[n * plan.height : (n + 1) * plan.height, :], whole, NT, preferred_element_type=jnp.float32
            )
            out_vmem[at, :] = slab_ref[at, :] - product
            copy = pltpu.make_async_copy(out_vmem.at[at, :], next_ref.at[at, :], sems.at[len(copies)])
            copy.start()
            copies.append(copy)
    for copy in copies:
        copy.wait()


def update(plan, groups, solved, mine, other, slab):
    vmem = pl.BlockSpec(memory_space=pltpu.VMEM)
    return pl.pallas_call(
        functools.partial(update_kernel, plan, groups, len(solved)),
        out_shape=jax.ShapeDtypeStruct(slab.shape, jnp.float32),
        in_specs=[vmem] * (len(solved) + 3),
        out_specs=pl.BlockSpec(memory_space=pl.ANY),
        scratch_shapes=[
            pltpu.VMEM((plan.total, mine.shape[1]), jnp.bfloat16),
            pltpu.VMEM(slab.shape, jnp.float32),
            pltpu.SemaphoreType.DMA((plan.pcols,)),
        ],
        cost_estimate=pl.CostEstimate(flops=300_000_000, bytes_accessed=8 * slab.size, transcendentals=0),
        compiler_params=pltpu.CompilerParams(vmem_limit_bytes=8 << 20),
        name="update",
    )(*solved, mine, other, slab)


def per_device(diag_block, panel, slab):
    prows = lax.axis_size("prow")
    pcols = lax.axis_size("pcol")
    width = diag_block.shape[0]
    plan = Plan(prows, pcols, width, panel.shape[0], slab.shape[1] // width)
    row, me = lax.axis_index("prow"), lax.axis_index("pcol")
    both = ("prow", "pcol")
    partner = [(i, i ^ 1) for i in range(pcols)]
    pieces = [panel]
    for j in range(1, plan.slots):
        pieces.append(lax.ppermute(panel, both, plan.pairs(j)))
    inverse = inverse_factor(diag_block)
    early, passed, factored = solve_pieces(plan, inverse, pieces[: plan.early], True)
    received = [passed]
    for k in range(1, prows):
        received.append(lax.ppermute(passed, both, plan.pass_on(k)))
    solved = [early]
    groups = [(tuple(range(plan.early)), 0)]
    if plan.early < plan.slots:
        (late,) = solve_pieces(plan, inverse, pieces[plan.early :], False)
        solved.append(late)
        groups.append((tuple(range(plan.early, plan.slots)), 0))
    for x, (slots, _) in zip(list(solved), list(groups)):
        solved.append(lax.ppermute(x, "pcol", partner))
        groups.append((slots, 1))

    def part(column):
        found = received[0]
        source = row ^ lax.rem(column, prows)
        for k in range(1, prows):
            found = jnp.where(source == k, received[k], found)
        return found

    mine = part(me)
    other = lax.ppermute(part(me ^ 1), "pcol", partner)
    slab_next = update(plan, groups, solved, mine, other, slab)
    return slab_next, factored


def solution(mesh):
    placed = (P(), P(("prow", "pcol"), None), P("prow", "pcol"))
    return jax.shard_map(
        per_device,
        mesh=mesh,
        in_specs=placed,
        out_specs=(P("prow", "pcol"), P(("prow", "pcol"), None)),
        check_vma=False,
    )
```

```python
import functools

import jax
import jax.numpy as jnp
from jax import lax
from jax.experimental import pallas as pl
from jax.experimental.pallas import tpu as pltpu
from jax.sharding import PartitionSpec as P


GROUP = 8
EXACT = lax.Precision.HIGHEST
NT = (((1,), (1,)), ((), ()))


def invert_factor(diag_ref, out_ref):
    n = diag_ref.shape[0]
    lane = lax.broadcasted_iota(jnp.int32, (GROUP, n), 1)
    sub = lax.broadcasted_iota(jnp.int32, (GROUP, n), 0)
    rows = [diag_ref[i : i + GROUP, :] for i in range(0, n, GROUP)]

    def column(x, at):
        return jnp.broadcast_to(x[:, at : at + 1], (GROUP, n))

    def row(x, at):
        return jnp.broadcast_to(x[at : at + 1, :], (GROUP, n))

    for b in range(n // GROUP):
        first = b * GROUP
        inside = (lane >= first) & (lane < first + GROUP)
        cols = [column(rows[b], first + j) for j in range(GROUP)]
        work = jnp.where(inside, jnp.where(lane - first == sub, 1.0, 0.0), rows[b])
        scale, scaled, cross = [], [], {}
        for k in range(GROUP):
            scale.append(lax.rsqrt(row(cols[k], k)))
            scaled.append(row(work, k) * scale[k])
            if k < GROUP - 1:
                factor = jnp.where(sub > k, cols[k] * scale[k], 0.0)
                for j in range(k + 1, GROUP):
                    cross[k, j] = row(cols[j], k) * scale[k]
                    cols[j] = cols[j] - factor * cross[k, j]
                work = work - factor * scaled[k]
        done = scaled[0]
        for k in range(1, GROUP):
            done = jnp.where(sub == k, scaled[k], done)
        out_ref[first : first + GROUP, :] = jnp.where(lane <= sub + first, done, 0.0)
        for i in range(b + 1, n // GROUP):
            cols = [column(rows[i], first + j) for j in range(GROUP)]
            rest = jnp.where(inside, 0.0, rows[i])
            for k in range(GROUP):
                factor = cols[k] * scale[k]
                for j in range(k + 1, GROUP):
                    cols[j] = cols[j] - factor * cross[k, j]
                rest = rest - factor * scaled[k]
            rows[i] = rest


def solve_kernel(diag_ref, panel_ref, factored_ref, low_ref, inverse):
    invert_factor(diag_ref, inverse)
    solved = lax.dot_general(
        panel_ref[...], inverse[...], NT, precision=EXACT, preferred_element_type=jnp.float32
    )
    factored_ref[...] = solved
    low_ref[...] = solved.astype(jnp.bfloat16)


def solve_panel(diag_block, panel):
    vmem = pl.BlockSpec(memory_space=pltpu.VMEM)
    return pl.pallas_call(
        solve_kernel,
        out_shape=(
            jax.ShapeDtypeStruct(panel.shape, jnp.float32),
            jax.ShapeDtypeStruct(panel.shape, jnp.bfloat16),
        ),
        in_specs=[vmem, vmem],
        out_specs=(vmem, vmem),
        scratch_shapes=[pltpu.VMEM(diag_block.shape, jnp.float32)],
        cost_estimate=pl.CostEstimate(flops=2_000_000_000, bytes_accessed=8 * panel.size, transcendentals=0),
        compiler_params=pltpu.CompilerParams(vmem_limit_bytes=2 << 20),
        name="solve_panel",
    )(diag_block, panel)


class Plan:
    def __init__(self, prows, pcols, width, height, here):
        self.prows, self.pcols, self.height = prows, pcols, height
        self.step = min(width, height)
        spread = pcols // prows

        def strips(column):
            found = []
            for position in range(here):
                block = column // prows + position * spread
                for offset in range(0, width, self.step):
                    at = block * width + offset
                    found.append((at // height, at % height))
            return found

        self.total = here * width
        parity = [shard % 2 for shard, _ in strips(0)]
        assert parity == [s % 2 for s in range(len(parity))]
        self.strips_each = len(parity) // 2
        self.slots = pcols // 2
        self.flips = []
        for row in range(prows):
            first = []
            for column in range(row, pcols, prows):
                for shard, _ in strips(column):
                    k = 2 * ((shard // 2) ^ (column // 2))
                    if k and k not in first:
                        first.append(k)
            first.sort(reverse=True)
            rest = [k for k in range(2, pcols, 2) if k not in first]
            self.flips.append([0] + first + rest)
        self.places = [[None] * (prows * pcols) for _ in range(self.strips_each)]
        for row in range(prows):
            for me in range(pcols):
                for column in (me, me ^ 1):
                    if column % prows == row:
                        own = [s for s in strips(column) if s[0] % 2 == me % 2]
                        for n, (shard, at) in enumerate(own):
                            slot = self.flips[row].index(2 * ((shard // 2) ^ (me // 2)))
                            self.places[n][row * pcols + me] = (slot, at)

    def pairs(self, slot):
        return [
            (row * self.pcols + i, row * self.pcols + (i ^ self.flips[row][slot]))
            for row in range(self.prows)
            for i in range(self.pcols)
        ]


def pick(values, index):
    chosen = jnp.int32(values[0])
    for i, value in enumerate(values[1:], 1):
        chosen = jnp.where(index == i, jnp.int32(value), chosen)
    return chosen


def update_kernel(plan, count, *refs):
    x_refs, refs = refs[:count], refs[count:]
    mine_ref, other_ref, slab_ref, next_ref, column, out_vmem, sems = refs
    row, me = lax.axis_index("prow"), lax.axis_index("pcol")
    parity = lax.rem(me, 2)
    step = plan.step
    for s in range(plan.strips_each):
        for ref, side in ((mine_ref, parity), (other_ref, 1 - parity)):
            at = pl.multiple_of((2 * s + side) * step, step)
            column[pl.ds(at, step), :] = ref[s * step : (s + 1) * step, :]
    whole = column[...]
    flips = [pick([f[j] for f in plan.flips], row) for j in range(plan.slots)]
    copies = []
    for n, ref in enumerate(x_refs):
        from_column = me ^ flips[n % plan.slots] ^ (n // plan.slots)
        at = pl.ds(pl.multiple_of(from_column * plan.height, plan.height), plan.height)
        product = lax.dot_general(ref[...], whole, NT, preferred_element_type=jnp.float32)
        out_vmem[at, :] = slab_ref[at, :] - product
        copy = pltpu.make_async_copy(out_vmem.at[at, :], next_ref.at[at, :], sems.at[n])
        copy.start()
        copies.append(copy)
    for copy in copies:
        copy.wait()


def update(plan, solved, mine, other, slab):
    vmem = pl.BlockSpec(memory_space=pltpu.VMEM)
    return pl.pallas_call(
        functools.partial(update_kernel, plan, len(solved)),
        out_shape=jax.ShapeDtypeStruct(slab.shape, jnp.float32),
        in_specs=[vmem] * (len(solved) + 3),
        out_specs=pl.BlockSpec(memory_space=pl.ANY),
        scratch_shapes=[
            pltpu.VMEM((plan.total, mine.shape[1]), jnp.bfloat16),
            pltpu.VMEM(slab.shape, jnp.float32),
            pltpu.SemaphoreType.DMA((plan.pcols,)),
        ],
        cost_estimate=pl.CostEstimate(flops=300_000_000, bytes_accessed=8 * slab.size, transcendentals=0),
        compiler_params=pltpu.CompilerParams(vmem_limit_bytes=8 << 20),
        name="update",
    )(*solved, mine, other, slab)


def choose(options, index):
    chosen = options[0][0]
    for value, indices in options[1:]:
        hit = index == indices[0]
        for i in indices[1:]:
            hit = hit | (index == i)
        chosen = jnp.where(hit, value, chosen)
    return chosen


def per_device(diag_block, panel, slab):
    prows = lax.axis_size("prow")
    pcols = lax.axis_size("pcol")
    width = diag_block.shape[0]
    plan = Plan(prows, pcols, width, panel.shape[0], slab.shape[1] // width)
    row, me = lax.axis_index("prow"), lax.axis_index("pcol")
    device = row * pcols + me
    both = ("prow", "pcol")
    partner = [(i, i ^ 1) for i in range(pcols)]
    factored, low = solve_panel(diag_block, panel)
    solved = [low]
    for j in range(1, plan.slots):
        solved.append(lax.ppermute(low, both, plan.pairs(j)))

    strips = []
    for places in plan.places:
        options = {}
        for at, place in enumerate(places):
            if place is not None:
                options.setdefault(place, []).append(at)
        strips.append(choose([(solved[j][at : at + plan.step], where) for (j, at), where in options.items()], device))
    passed = jnp.concatenate(strips, 0) if len(strips) > 1 else strips[0]
    received = [(passed, [0])]
    for k in range(1, prows):
        received.append((lax.ppermute(passed, "prow", [(i, i ^ k) for i in range(prows)]), [k]))
    for j in range(plan.slots):
        solved.append(lax.ppermute(solved[j], "pcol", partner))
    mine = choose(received, row ^ lax.rem(me, prows))
    other = lax.ppermute(choose(received, row ^ lax.rem(me ^ 1, prows)), "pcol", partner)
    slab_next = update(plan, solved, mine, other, slab)
    return slab_next, factored


def solution(mesh):
    placed = (P(), P(("prow", "pcol"), None), P("prow", "pcol"))
    return jax.shard_map(
        per_device,
        mesh=mesh,
        in_specs=placed,
        out_specs=(P("prow", "pcol"), P(("prow", "pcol"), None)),
        check_vma=False,
    )
```

```python
import functools

import jax
import jax.numpy as jnp
from jax import lax
from jax.experimental import pallas as pl
from jax.experimental.pallas import tpu as pltpu
from jax.sharding import PartitionSpec as P


GROUP = 8
LANES = 128
EXACT = lax.Precision.HIGHEST
NT = (((1,), (1,)), ((), ()))


def invert_factor(diag_ref, out_ref):
    n = diag_ref.shape[0]
    groups = n // GROUP
    lane = lax.broadcasted_iota(jnp.int32, (GROUP, n), 1)
    sub = lax.broadcasted_iota(jnp.int32, (GROUP, n), 0)
    rows = [diag_ref[i * GROUP : (i + 1) * GROUP, :] for i in range(groups)]
    zero = jnp.where(lane >= n, rows[0], 0.0)

    def columns(x, first):
        return [jnp.broadcast_to(x[:, at : at + 1], (GROUP, n)) for at in range(first, first + GROUP)]

    def row(x, at):
        return jnp.broadcast_to(x[at : at + 1, :], (GROUP, n))

    cols = [c + zero for c in columns(rows[0], 0)]
    for b in range(groups):
        first = b * GROUP
        inside = (lane >= first) & (lane < first + GROUP)
        work = jnp.where(inside, jnp.where(lane - first == sub, 1.0, 0.0), rows[b])
        scale, scaled, cross = [], [], {}
        follows = b + 1 < groups
        if follows:
            below = columns(rows[b + 1], first)
            ahead = [c + zero for c in columns(rows[b + 1], first + GROUP)]
            rest = jnp.where(inside, 0.0, rows[b + 1])
        for k in range(GROUP):
            scale.append(lax.rsqrt(row(cols[k], k)))
            scaled.append(row(work, k) * scale[k])
            if k < GROUP - 1:
                factor = jnp.where(sub > k, cols[k], 0.0) * scale[k]
                for j in range(k + 1, GROUP):
                    cross[k, j] = row(cols[j], k) * scale[k]
                    cols[j] = cols[j] - factor * cross[k, j]
                work = work - factor * scaled[k]
            if follows:
                factor = below[k] * scale[k]
                for j in range(k + 1, GROUP):
                    below[j] = below[j] - factor * cross[k, j]
                rest = rest - factor * scaled[k]
                for j in range(GROUP):
                    ahead[j] = ahead[j] - factor * row(factor, j)
        done = scaled[0]
        for k in range(1, GROUP):
            done = jnp.where(sub == k, scaled[k], done)
        out_ref[first : first + GROUP, :] = jnp.where(lane <= sub + first, done, 0.0)
        if follows:
            cols = ahead
            rows[b + 1] = rest
        for i in range(b + 2, groups):
            below = columns(rows[i], first)
            rest = jnp.where(inside, 0.0, rows[i])
            for k in range(GROUP):
                factor = below[k] * scale[k]
                for j in range(k + 1, GROUP):
                    below[j] = below[j] - factor * cross[k, j]
                rest = rest - factor * scaled[k]
            rows[i] = rest


def inverse_factor(diag_block):
    vmem = pl.BlockSpec(memory_space=pltpu.VMEM)
    return pl.pallas_call(
        invert_factor,
        out_shape=jax.ShapeDtypeStruct(diag_block.shape, jnp.float32),
        in_specs=[vmem],
        out_specs=vmem,
        cost_estimate=pl.CostEstimate(flops=2_000_000_000, bytes_accessed=8 * diag_block.size, transcendentals=0),
        compiler_params=pltpu.CompilerParams(vmem_limit_bytes=2 << 20),
        name="inverse_factor",
    )(diag_block)


def solve_kernel(inverse_ref, panel_ref, solved_ref, low_ref):
    solved = lax.dot_general(
        panel_ref[...], inverse_ref[...], NT, precision=EXACT, preferred_element_type=jnp.float32
    )
    low_ref[...] = solved.astype(jnp.bfloat16)
    solved_ref[...] = solved


def solve_panel(diag_block, panel):
    vmem = pl.BlockSpec(memory_space=pltpu.VMEM)
    return pl.pallas_call(
        solve_kernel,
        out_shape=(
            jax.ShapeDtypeStruct(panel.shape, jnp.float32),
            jax.ShapeDtypeStruct(panel.shape, jnp.bfloat16),
        ),
        in_specs=[vmem, vmem],
        out_specs=(vmem, vmem),
        cost_estimate=pl.CostEstimate(flops=200_000_000, bytes_accessed=8 * panel.size, transcendentals=0),
        compiler_params=pltpu.CompilerParams(vmem_limit_bytes=2 << 20),
        name="solve_panel",
    )(inverse_factor(diag_block), panel)


class Plan:
    def __init__(self, prows, pcols, width, height, here):
        self.prows, self.pcols, self.height = prows, pcols, height
        self.step = min(width, height)
        spread = pcols // prows

        def strips(column):
            found = []
            for position in range(here):
                block = column // prows + position * spread
                for offset in range(0, width, self.step):
                    at = block * width + offset
                    found.append((at // height, at % height))
            return found

        self.total = here * width
        parity = [shard % 2 for shard, _ in strips(0)]
        assert parity == [s % 2 for s in range(len(parity))]
        self.strips_each = len(parity) // 2
        self.slots = pcols // 2
        self.flips = []
        for row in range(prows):
            first = []
            for column in range(row, pcols, prows):
                for shard, _ in strips(column):
                    k = 2 * ((shard // 2) ^ (column // 2))
                    if k and k not in first:
                        first.append(k)
            first.sort(reverse=True)
            rest = [k for k in range(2, pcols, 2) if k not in first]
            self.flips.append([0] + first + rest)
        self.places = [[None] * (prows * pcols) for _ in range(self.strips_each)]
        for row in range(prows):
            for me in range(pcols):
                for column in (me, me ^ 1):
                    if column % prows == row:
                        own = [s for s in strips(column) if s[0] % 2 == me % 2]
                        for n, (shard, at) in enumerate(own):
                            slot = self.flips[row].index(2 * ((shard // 2) ^ (me // 2)))
                            self.places[n][row * pcols + me] = (slot, at)

    def pairs(self, slot):
        return [
            (row * self.pcols + i, row * self.pcols + (i ^ self.flips[row][slot]))
            for row in range(self.prows)
            for i in range(self.pcols)
        ]


def pick(values, index):
    chosen = jnp.int32(values[0])
    for i, value in enumerate(values[1:], 1):
        chosen = jnp.where(index == i, jnp.int32(value), chosen)
    return chosen


def update_kernel(plan, count, sides, aliased, *refs):
    x_refs, refs = refs[:count], refs[count:]
    strip_refs, refs = refs[: len(sides)], refs[len(sides) :]
    if aliased:
        slab_ref, _, next_ref, column, out_vmem, sems = refs
    else:
        slab_ref, solved_ref, next_ref, factored_ref, column, out_vmem, sems = refs
        factored_copy = pltpu.make_async_copy(solved_ref, factored_ref, sems.at[count])
        factored_copy.start()
    row, me = lax.axis_index("prow"), lax.axis_index("pcol")
    parity = lax.rem(me, 2)
    step = plan.step
    across = pl.ds(0, plan.total)
    if len(sides) == 1:
        across = pl.ds(pl.multiple_of((parity ^ sides[0]) * step, step), step)
        whole = strip_refs[0][...]
    else:
        for s in range(plan.strips_each):
            for ref, side in zip(strip_refs, sides):
                at = pl.multiple_of((2 * s + (parity ^ side)) * step, step)
                column[pl.ds(at, step), :] = ref[s * step : (s + 1) * step, :]
        whole = column[...]
    flips = [pick([f[j] for f in plan.flips], row) for j in range(plan.slots)]
    copies = []
    for n, ref in enumerate(x_refs):
        from_column = me ^ flips[n % plan.slots] ^ (n // plan.slots)
        at = pl.ds(pl.multiple_of(from_column * plan.height, plan.height), plan.height)
        product = lax.dot_general(ref[...], whole, NT, preferred_element_type=jnp.float32)
        out_vmem[at, :] = slab_ref[at, across] - product
        copy = pltpu.make_async_copy(out_vmem.at[at, :], next_ref.at[at, across], sems.at[n])
        copy.start()
        copies.append(copy)
    if not aliased:
        copies.append(factored_copy)
    for copy in copies:
        copy.wait()


def update(plan, solved, strips, sides, slab, own, previous):
    vmem, hbm = pl.BlockSpec(memory_space=pltpu.VMEM), pl.BlockSpec(memory_space=pltpu.HBM)
    aliased = previous is not None
    wide = plan.step * plan.strips_each * len(sides)
    operands = [*solved, *strips, slab, previous if aliased else own]
    outs, out_specs = [jax.ShapeDtypeStruct(slab.shape, jnp.float32)], [hbm]
    if not aliased:
        outs.append(jax.ShapeDtypeStruct(own.shape, jnp.float32))
        out_specs.append(hbm)
    return pl.pallas_call(
        functools.partial(update_kernel, plan, len(solved), sides, aliased),
        out_shape=tuple(outs),
        in_specs=[vmem] * (len(operands) - 1) + [hbm if aliased else vmem],
        out_specs=tuple(out_specs),
        scratch_shapes=[
            pltpu.VMEM((plan.total, own.shape[1]), jnp.bfloat16),
            pltpu.VMEM((slab.shape[0], wide), jnp.float32),
            pltpu.SemaphoreType.DMA((plan.pcols + 1,)),
        ],
        input_output_aliases={len(operands) - 1: 0} if aliased else {},
        cost_estimate=pl.CostEstimate(flops=300_000_000, bytes_accessed=8 * slab.size, transcendentals=0),
        compiler_params=pltpu.CompilerParams(vmem_limit_bytes=8 << 20),
        name="update_rest" if aliased else "update",
    )(*operands)


def choose(options, index):
    chosen = options[0][0]
    for value, indices in options[1:]:
        hit = index == indices[0]
        for i in indices[1:]:
            hit = hit | (index == i)
        chosen = jnp.where(hit, value, chosen)
    return chosen


def per_device(diag_block, panel, slab):
    prows = lax.axis_size("prow")
    pcols = lax.axis_size("pcol")
    width = diag_block.shape[0]
    plan = Plan(prows, pcols, width, panel.shape[0], slab.shape[1] // width)
    row, me = lax.axis_index("prow"), lax.axis_index("pcol")
    device = row * pcols + me
    both = ("prow", "pcol")
    partner = [(i, i ^ 1) for i in range(pcols)]
    own, low = solve_panel(diag_block, panel)
    solved = [low]
    for j in range(1, plan.slots):
        solved.append(lax.ppermute(low, both, plan.pairs(j)))

    strips = []
    for places in plan.places:
        options = {}
        for at, place in enumerate(places):
            if place is not None:
                options.setdefault(place, []).append(at)
        strips.append(choose([(solved[j][at : at + plan.step], where) for (j, at), where in options.items()], device))
    passed = jnp.concatenate(strips, 0) if len(strips) > 1 else strips[0]
    received = [(passed, [0])]
    for k in range(1, prows):
        received.append((lax.ppermute(passed, "prow", [(i, i ^ k) for i in range(prows)]), [k]))
    for j in range(plan.slots):
        solved.append(lax.ppermute(solved[j], "pcol", partner))
    mine = choose(received, row ^ lax.rem(me, prows))
    other = lax.ppermute(choose(received, row ^ lax.rem(me ^ 1, prows)), "pcol", partner)
    if plan.strips_each == 1 and plan.step % LANES == 0:
        slab_next, factored = update(plan, solved, [mine], (0,), slab, own, None)
        (slab_next,) = update(plan, solved, [other], (1,), slab, own, slab_next)
    else:
        slab_next, factored = update(plan, solved, [mine, other], (0, 1), slab, own, None)
    return slab_next, factored


def solution(mesh):
    placed = (P(), P(("prow", "pcol"), None), P("prow", "pcol"))
    return jax.shard_map(
        per_device,
        mesh=mesh,
        in_specs=placed,
        out_specs=(P("prow", "pcol"), P(("prow", "pcol"), None)),
        check_vma=False,
    )
```

```python
import functools

import jax
import jax.numpy as jnp
from jax import lax
from jax.experimental import pallas as pl
from jax.experimental.pallas import tpu as pltpu
from jax.sharding import PartitionSpec as P


GROUP = 8
LANES = 128
FAR = (-1, 0)
EXACT = lax.Precision.HIGHEST
NT = (((1,), (1,)), ((), ()))


def invert_factor(diag_ref, out_ref):
    n = diag_ref.shape[0]
    groups = n // GROUP
    lane = lax.broadcasted_iota(jnp.int32, (GROUP, n), 1)
    sub = lax.broadcasted_iota(jnp.int32, (GROUP, n), 0)
    rows = [diag_ref[i * GROUP : (i + 1) * GROUP, :] for i in range(groups)]
    zero = jnp.where(lane >= n, rows[0], 0.0)

    def columns(x, first):
        return [jnp.broadcast_to(x[:, at : at + 1], (GROUP, n)) for at in range(first, first + GROUP)]

    def row(x, at):
        return jnp.broadcast_to(x[at : at + 1, :], (GROUP, n))

    cols = [c + zero for c in columns(rows[0], 0)]
    for b in range(groups):
        first = b * GROUP
        inside = (lane >= first) & (lane < first + GROUP)
        work = jnp.where(inside, jnp.where(lane - first == sub, 1.0, 0.0), rows[b])
        scale, scaled, cross = [], [], {}
        follows = b + 1 < groups
        if follows:
            below = columns(rows[b + 1], first)
            ahead = [c + zero for c in columns(rows[b + 1], first + GROUP)]
            rest = jnp.where(inside, 0.0, rows[b + 1])
        for k in range(GROUP):
            scale.append(lax.rsqrt(row(cols[k], k)))
            scaled.append(row(work, k) * scale[k])
            if k < GROUP - 1:
                factor = jnp.where(sub > k, cols[k], 0.0) * scale[k]
                for j in range(k + 1, GROUP):
                    cross[k, j] = row(cols[j], k) * scale[k]
                    cols[j] = cols[j] - factor * cross[k, j]
                work = work - factor * scaled[k]
            if follows:
                factor = below[k] * scale[k]
                for j in range(k + 1, GROUP):
                    below[j] = below[j] - factor * cross[k, j]
                rest = rest - factor * scaled[k]
                for j in range(GROUP):
                    ahead[j] = ahead[j] - factor * row(factor, j)
        done = scaled[0]
        for k in range(1, GROUP):
            done = jnp.where(sub == k, scaled[k], done)
        out_ref[first : first + GROUP, :] = jnp.where(lane <= sub + first, done, 0.0)
        if follows:
            cols = ahead
            rows[b + 1] = rest
        for i in range(b + 2, groups):
            below = columns(rows[i], first)
            rest = jnp.where(inside, 0.0, rows[i])
            for k in range(GROUP):
                factor = below[k] * scale[k]
                for j in range(k + 1, GROUP):
                    below[j] = below[j] - factor * cross[k, j]
                rest = rest - factor * scaled[k]
            rows[i] = rest


def only_for(devices, wanted, body):
    me = lax.axis_index("pcol")
    listed = functools.reduce(jnp.logical_or, [me == i for i in devices])
    pl.when(listed if wanted else jnp.logical_not(listed))(body)


def solve_rows(inverse_ref, rows, solved_ref, low_ref):
    solved = lax.dot_general(rows[...], inverse_ref[...], NT, precision=EXACT, preferred_element_type=jnp.float32)
    low_ref[...] = solved.astype(jnp.bfloat16)
    solved_ref[...] = solved


def first_kernel(devices, diag_hbm, panel_hbm, solved_ref, low_ref, diag, panel, inverse, sems):
    def body():
        diag_copy = pltpu.make_async_copy(diag_hbm, diag, sems.at[0])
        panel_copy = pltpu.make_async_copy(panel_hbm, panel, sems.at[1])
        diag_copy.start()
        panel_copy.start()
        diag_copy.wait()
        invert_factor(diag, inverse)
        panel_copy.wait()
        solve_rows(inverse, panel, solved_ref, low_ref)

    only_for(devices, True, body)


def rest_kernel(devices, panel_hbm, diag_ref, _, __, solved_ref, low_ref, panel, inverse, sems):
    def body():
        panel_copy = pltpu.make_async_copy(panel_hbm, panel, sems.at[0])
        panel_copy.start()
        invert_factor(diag_ref, inverse)
        panel_copy.wait()
        solve_rows(inverse, panel, solved_ref, low_ref)

    only_for(devices, False, body)


def solve_panel(diag_block, panel, devices, before):
    vmem, hbm = pl.BlockSpec(memory_space=pltpu.VMEM), pl.BlockSpec(memory_space=pl.ANY)
    panel_hbm = pltpu.with_memory_space_constraint(panel, pltpu.HBM)
    if before:
        operands, in_specs = (panel_hbm, diag_block, *before), [hbm, vmem, vmem, vmem]
    else:
        operands = (pltpu.with_memory_space_constraint(diag_block, pltpu.HBM), panel_hbm)
        in_specs = [hbm, hbm]
    return pl.pallas_call(
        functools.partial(rest_kernel if before else first_kernel, devices),
        out_shape=(
            jax.ShapeDtypeStruct(panel.shape, jnp.float32),
            jax.ShapeDtypeStruct(panel.shape, jnp.bfloat16),
        ),
        in_specs=in_specs,
        out_specs=(vmem, vmem),
        scratch_shapes=([] if before else [pltpu.VMEM(diag_block.shape, jnp.float32)])
        + [
            pltpu.VMEM(panel.shape, jnp.float32),
            pltpu.VMEM(diag_block.shape, jnp.float32),
            pltpu.SemaphoreType.DMA((2,)),
        ],
        input_output_aliases={2: 0, 3: 1} if before else {},
        cost_estimate=pl.CostEstimate(flops=2_000_000_000, bytes_accessed=8 * panel.size, transcendentals=0),
        compiler_params=pltpu.CompilerParams(vmem_limit_bytes=2 << 20),
        name="solve_rest" if before else "solve_first",
    )(*operands)


class Plan:
    def __init__(self, prows, pcols, width, height, here):
        self.prows, self.pcols, self.height = prows, pcols, height
        self.step = min(width, height)
        spread = pcols // prows

        def strips(column):
            found = []
            for position in range(here):
                block = column // prows + position * spread
                for offset in range(0, width, self.step):
                    at = block * width + offset
                    found.append((at // height, at % height))
            return found

        self.total = here * width
        parity = [shard % 2 for shard, _ in strips(0)]
        assert parity == [s % 2 for s in range(len(parity))]
        self.strips_each = len(parity) // 2
        self.slots = pcols // 2
        self.far = {}
        if self.strips_each == 1:
            for row in range(min(prows, pcols)):
                column = max(range(row, pcols, prows))
                (even, at), (odd, same) = strips(column)
                if at == same and even // 2 == odd // 2 != column // 2:
                    self.far[row] = (column, even // 2, at)
        if len(self.far) < prows or len({at for _, _, at in self.far.values()}) > 1:
            self.far = {}
        self.sources = sorted({2 * chip + t for _, chip, _ in self.far.values() for t in range(2)})
        if not self.far:
            self.sources = range(pcols)
        self.flips = []
        for row in range(prows):
            first = []
            for column in range(row, pcols, prows):
                if self.far and column == self.far[row][0]:
                    continue
                for shard, _ in strips(column):
                    k = 2 * ((shard // 2) ^ (column // 2))
                    if k and k not in first:
                        first.append(k)
            first.sort(reverse=True)
            rest = [k for k in range(pcols - 2, 0, -2) if k not in first]
            if self.far and not first:
                first, rest = rest[-1:], rest[:-1]
            self.flips.append([0] + first + rest)
        self.places = [[None] * (prows * pcols) for _ in range(self.strips_each)]
        for row in range(prows):
            for me in range(pcols):
                for column in (me, me ^ 1):
                    if column % prows == row:
                        if self.far and column == self.far[row][0]:
                            self.places[0][row * pcols + me] = FAR
                            continue
                        own = [s for s in strips(column) if s[0] % 2 == me % 2]
                        for n, (shard, at) in enumerate(own):
                            slot = self.flips[row].index(2 * ((shard // 2) ^ (me // 2)))
                            self.places[n][row * pcols + me] = (slot, at)

    def far_pairs(self):
        return [
            (row * self.pcols + 2 * chip + t, row * self.pcols + (column // 2) * 2 + t)
            for row, (column, chip, _) in self.far.items()
            for t in range(2)
        ]

    def pairs(self, slot):
        return [
            (row * self.pcols + i, row * self.pcols + (i ^ self.flips[row][slot]))
            for row in range(self.prows)
            for i in range(self.pcols)
        ]


def pick(values, index):
    chosen = jnp.int32(values[0])
    for i, value in enumerate(values[1:], 1):
        chosen = jnp.where(index == i, jnp.int32(value), chosen)
    return chosen


def update_kernel(plan, count, sides, aliased, *refs):
    x_refs, refs = refs[:count], refs[count:]
    strip_refs, refs = refs[: len(sides)], refs[len(sides) :]
    if aliased:
        slab_ref, _, next_ref, column, out_vmem, sems = refs
    else:
        slab_ref, solved_ref, next_ref, factored_ref, column, out_vmem, sems = refs
        factored_copy = pltpu.make_async_copy(solved_ref, factored_ref, sems.at[count])
        factored_copy.start()
    row, me = lax.axis_index("prow"), lax.axis_index("pcol")
    parity = lax.rem(me, 2)
    step = plan.step
    across = pl.ds(0, plan.total)
    if len(sides) == 1:
        across = pl.ds(pl.multiple_of((parity ^ sides[0]) * step, step), step)
        whole = strip_refs[0][...]
    else:
        for s in range(plan.strips_each):
            for ref, side in zip(strip_refs, sides):
                at = pl.multiple_of((2 * s + (parity ^ side)) * step, step)
                column[pl.ds(at, step), :] = ref[s * step : (s + 1) * step, :]
        whole = column[...]
    flips = [pick([f[j] for f in plan.flips], row) for j in range(plan.slots)]
    copies = []
    for n, ref in enumerate(x_refs):
        from_column = me ^ flips[n % plan.slots] ^ (n // plan.slots)
        at = pl.ds(pl.multiple_of(from_column * plan.height, plan.height), plan.height)
        product = lax.dot_general(ref[...], whole, NT, preferred_element_type=jnp.float32)
        out_vmem[at, :] = slab_ref[at, across] - product
        copy = pltpu.make_async_copy(out_vmem.at[at, :], next_ref.at[at, across], sems.at[n])
        copy.start()
        copies.append(copy)
    if not aliased:
        copies.append(factored_copy)
    for copy in copies:
        copy.wait()


def update(plan, solved, strips, sides, slab, own, previous):
    vmem, hbm = pl.BlockSpec(memory_space=pltpu.VMEM), pl.BlockSpec(memory_space=pltpu.HBM)
    aliased = previous is not None
    wide = plan.step * plan.strips_each * len(sides)
    operands = [*solved, *strips, slab, previous if aliased else own]
    outs, out_specs = [jax.ShapeDtypeStruct(slab.shape, jnp.float32)], [hbm]
    if not aliased:
        outs.append(jax.ShapeDtypeStruct(own.shape, jnp.float32))
        out_specs.append(hbm)
    return pl.pallas_call(
        functools.partial(update_kernel, plan, len(solved), sides, aliased),
        out_shape=tuple(outs),
        in_specs=[vmem] * (len(operands) - 1) + [hbm if aliased else vmem],
        out_specs=tuple(out_specs),
        scratch_shapes=[
            pltpu.VMEM((plan.total, own.shape[1]), jnp.bfloat16),
            pltpu.VMEM((slab.shape[0], wide), jnp.float32),
            pltpu.SemaphoreType.DMA((plan.pcols + 1,)),
        ],
        input_output_aliases={len(operands) - 1: 0} if aliased else {},
        cost_estimate=pl.CostEstimate(flops=300_000_000, bytes_accessed=8 * slab.size, transcendentals=0),
        compiler_params=pltpu.CompilerParams(vmem_limit_bytes=8 << 20),
        name="update_rest" if aliased else "update",
    )(*operands)


def choose(options, index):
    chosen = options[0][0]
    for value, indices in options[1:]:
        hit = index == indices[0]
        for i in indices[1:]:
            hit = hit | (index == i)
        chosen = jnp.where(hit, value, chosen)
    return chosen


def per_device(diag_block, panel, slab):
    prows = lax.axis_size("prow")
    pcols = lax.axis_size("pcol")
    width = diag_block.shape[0]
    plan = Plan(prows, pcols, width, panel.shape[0], slab.shape[1] // width)
    row, me = lax.axis_index("prow"), lax.axis_index("pcol")
    device = row * pcols + me
    both = ("prow", "pcol")
    partner = [(i, i ^ 1) for i in range(pcols)]
    own, low = solve_panel(diag_block, panel, plan.sources, ())
    if plan.far:
        at = plan.far[0][2]
        far = lax.ppermute(low[at : at + plan.step], both, plan.far_pairs())
        own, low = solve_panel(diag_block, panel, plan.sources, (own, low))
    solved = [low]
    for j in range(1, plan.slots):
        solved.append(lax.ppermute(low, both, plan.pairs(j)))

    strips = []
    for places in plan.places:
        options = {}
        for at, place in enumerate(places):
            if place is not None:
                options.setdefault(place, []).append(at)
        strips.append(
            choose(
                [(far if j < 0 else solved[j][at : at + plan.step], where) for (j, at), where in options.items()],
                device,
            )
        )
    passed = jnp.concatenate(strips, 0) if len(strips) > 1 else strips[0]
    received = [(passed, [0])]
    for k in range(1, prows):
        received.append((lax.ppermute(passed, "prow", [(i, i ^ k) for i in range(prows)]), [k]))
    for j in range(plan.slots):
        solved.append(lax.ppermute(solved[j], "pcol", partner))
    mine = choose(received, row ^ lax.rem(me, prows))
    other = lax.ppermute(choose(received, row ^ lax.rem(me ^ 1, prows)), "pcol", partner)
    if plan.strips_each == 1 and plan.step % LANES == 0:
        slab_next, factored = update(plan, solved, [mine], (0,), slab, own, None)
        (slab_next,) = update(plan, solved, [other], (1,), slab, own, slab_next)
    else:
        slab_next, factored = update(plan, solved, [mine, other], (0, 1), slab, own, None)
    return slab_next, factored


def solution(mesh):
    placed = (P(), P(("prow", "pcol"), None), P("prow", "pcol"))
    return jax.shard_map(
        per_device,
        mesh=mesh,
        in_specs=placed,
        out_specs=(P("prow", "pcol"), P(("prow", "pcol"), None)),
        check_vma=False,
    )
```

```python
import functools

import jax
import jax.numpy as jnp
from jax import lax
from jax.experimental import pallas as pl
from jax.experimental.pallas import tpu as pltpu
from jax.sharding import PartitionSpec as P


GROUP = 8
LANES = 128
FAR = (-1, 0)
EXACT = lax.Precision.HIGHEST
NT = (((1,), (1,)), ((), ()))


def invert_factor(diag_ref, out_ref):
    n = diag_ref.shape[0]
    groups = n // GROUP
    lane = lax.broadcasted_iota(jnp.int32, (GROUP, n), 1)
    sub = lax.broadcasted_iota(jnp.int32, (GROUP, n), 0)
    rows = [diag_ref[i * GROUP : (i + 1) * GROUP, :] for i in range(groups)]
    zero = jnp.where(lane >= n, rows[0], 0.0)

    def columns(x, first):
        return [jnp.broadcast_to(x[:, at : at + 1], (GROUP, n)) for at in range(first, first + GROUP)]

    def row(x, at):
        return jnp.broadcast_to(x[at : at + 1, :], (GROUP, n))

    cols = [c + zero for c in columns(rows[0], 0)]
    for b in range(groups):
        first = b * GROUP
        inside = (lane >= first) & (lane < first + GROUP)
        work = jnp.where(inside, jnp.where(lane - first == sub, 1.0, 0.0), rows[b])
        scale, scaled, cross = [], [], {}
        follows = b + 1 < groups
        if follows:
            below = columns(rows[b + 1], first)
            ahead = [c + zero for c in columns(rows[b + 1], first + GROUP)]
            rest = jnp.where(inside, 0.0, rows[b + 1])
        for k in range(GROUP):
            scale.append(lax.rsqrt(row(cols[k], k)))
            scaled.append(row(work, k) * scale[k])
            if k < GROUP - 1:
                factor = jnp.where(sub > k, cols[k], 0.0) * scale[k]
                for j in range(k + 1, GROUP):
                    cross[k, j] = row(cols[j], k) * scale[k]
                    cols[j] = cols[j] - factor * cross[k, j]
                work = work - factor * scaled[k]
            if follows:
                factor = below[k] * scale[k]
                for j in range(k + 1, GROUP):
                    below[j] = below[j] - factor * cross[k, j]
                rest = rest - factor * scaled[k]
                for j in range(GROUP):
                    ahead[j] = ahead[j] - factor * row(factor, j)
        done = scaled[0]
        for k in range(1, GROUP):
            done = jnp.where(sub == k, scaled[k], done)
        out_ref[first : first + GROUP, :] = jnp.where(lane <= sub + first, done, 0.0)
        if follows:
            cols = ahead
            rows[b + 1] = rest
        for i in range(b + 2, groups):
            below = columns(rows[i], first)
            rest = jnp.where(inside, 0.0, rows[i])
            for k in range(GROUP):
                factor = below[k] * scale[k]
                for j in range(k + 1, GROUP):
                    below[j] = below[j] - factor * cross[k, j]
                rest = rest - factor * scaled[k]
            rows[i] = rest


def only_for(devices, wanted, body):
    me = lax.axis_index("pcol")
    listed = functools.reduce(jnp.logical_or, [me == i for i in devices])
    pl.when(listed if wanted else jnp.logical_not(listed))(body)


def solve_rows(inverse_ref, rows, solved_ref, low_ref):
    solved = lax.dot_general(rows[...], inverse_ref[...], NT, precision=EXACT, preferred_element_type=jnp.float32)
    low_ref[...] = solved.astype(jnp.bfloat16)
    solved_ref[...] = solved


def panel_kernel(devices, first, panel_hbm, diag_ref, _, *refs):
    inverse, solved_ref, low_ref, panel, sem = refs[-5:]

    def body():
        panel_copy = pltpu.make_async_copy(panel_hbm, panel, sem)
        panel_copy.start()
        invert_factor(diag_ref, inverse)
        panel_copy.wait()
        solve_rows(inverse, panel, solved_ref, low_ref)

    only_for(devices, first, body)


def mark_kernel(*refs):
    refs[-1][...] = jnp.zeros_like(refs[-1])


def mark(*before):
    vmem = pl.BlockSpec(memory_space=pltpu.VMEM)
    return pl.pallas_call(
        mark_kernel,
        out_shape=jax.ShapeDtypeStruct((GROUP, LANES), jnp.float32),
        in_specs=[vmem] * len(before),
        out_specs=vmem,
        cost_estimate=pl.CostEstimate(flops=400_000_000, bytes_accessed=4 * GROUP * LANES, transcendentals=0),
        compiler_params=pltpu.CompilerParams(vmem_limit_bytes=2 << 20),
        name="mark",
    )(*before)


def near_kernel(inverse_ref, rows_ref, low_ref):
    solved = lax.dot_general(
        rows_ref[...], inverse_ref[...], NT, precision=EXACT, preferred_element_type=jnp.float32
    )
    low_ref[...] = solved.astype(jnp.bfloat16)


def solve_near(inverse, rows):
    vmem = pl.BlockSpec(memory_space=pltpu.VMEM)
    return pl.pallas_call(
        near_kernel,
        out_shape=jax.ShapeDtypeStruct(rows.shape, jnp.bfloat16),
        in_specs=[vmem, vmem],
        out_specs=vmem,
        cost_estimate=pl.CostEstimate(flops=200_000_000, bytes_accessed=6 * rows.size, transcendentals=0),
        compiler_params=pltpu.CompilerParams(vmem_limit_bytes=2 << 20),
        name="solve_near",
    )(inverse, rows)


def solve_panel(diag_block, panel, opened, devices, before):
    vmem, hbm = pl.BlockSpec(memory_space=pltpu.VMEM), pl.BlockSpec(memory_space=pl.ANY)
    panel_hbm = pltpu.with_memory_space_constraint(panel, pltpu.HBM)
    return pl.pallas_call(
        functools.partial(panel_kernel, devices, not before),
        out_shape=(
            jax.ShapeDtypeStruct(diag_block.shape, jnp.float32),
            jax.ShapeDtypeStruct(panel.shape, jnp.float32),
            jax.ShapeDtypeStruct(panel.shape, jnp.bfloat16),
        ),
        in_specs=[hbm, vmem, vmem] + [vmem] * len(before),
        out_specs=(vmem, vmem, vmem),
        scratch_shapes=[pltpu.VMEM(panel.shape, jnp.float32), pltpu.SemaphoreType.DMA],
        input_output_aliases={3: 0, 4: 1, 5: 2} if before else {},
        cost_estimate=pl.CostEstimate(flops=2_000_000_000, bytes_accessed=8 * panel.size, transcendentals=0),
        compiler_params=pltpu.CompilerParams(vmem_limit_bytes=2 << 20),
        name="solve_rest" if before else "solve_first",
    )(panel_hbm, diag_block, opened, *before)


class Plan:
    def __init__(self, prows, pcols, width, height, here):
        self.prows, self.pcols, self.height = prows, pcols, height
        self.step = min(width, height)
        spread = pcols // prows

        def strips(column):
            found = []
            for position in range(here):
                block = column // prows + position * spread
                for offset in range(0, width, self.step):
                    at = block * width + offset
                    found.append((at // height, at % height))
            return found

        self.total = here * width
        parity = [shard % 2 for shard, _ in strips(0)]
        assert parity == [s % 2 for s in range(len(parity))]
        self.strips_each = len(parity) // 2
        self.slots = pcols // 2
        self.far = {}
        if self.strips_each == 1:
            for row in range(min(prows, pcols)):
                column = max(range(row, pcols, prows))
                (even, at), (odd, same) = strips(column)
                if at == same and even // 2 == odd // 2 != column // 2:
                    self.far[row] = (column, even // 2, at)
        if len(self.far) < prows or len({at for _, _, at in self.far.values()}) > 1:
            self.far = {}
        self.sources = sorted({2 * chip + t for _, chip, _ in self.far.values() for t in range(2)})
        if not self.far:
            self.sources = range(pcols)
        self.flips = []
        for row in range(prows):
            first = []
            for column in range(row, pcols, prows):
                if self.far and column == self.far[row][0]:
                    continue
                for shard, _ in strips(column):
                    k = 2 * ((shard // 2) ^ (column // 2))
                    if k and k not in first:
                        first.append(k)
            first.sort(reverse=True)
            rest = [k for k in range(pcols - 2, 0, -2) if k not in first]
            self.flips.append([0] + sorted(first + rest, key=lambda k: k != 2))
        self.places = [[None] * (prows * pcols) for _ in range(self.strips_each)]
        for row in range(prows):
            for me in range(pcols):
                for column in (me, me ^ 1):
                    if column % prows == row:
                        if self.far and column == self.far[row][0]:
                            self.places[0][row * pcols + me] = FAR
                            continue
                        own = [s for s in strips(column) if s[0] % 2 == me % 2]
                        for n, (shard, at) in enumerate(own):
                            slot = self.flips[row].index(2 * ((shard // 2) ^ (me // 2)))
                            self.places[n][row * pcols + me] = (slot, at)

    def far_pairs(self):
        return [
            (row * self.pcols + 2 * chip + t, row * self.pcols + (column // 2) * 2 + t)
            for row, (column, chip, _) in self.far.items()
            for t in range(2)
        ]

    def pairs(self, slot):
        return [
            (row * self.pcols + i, row * self.pcols + (i ^ self.flips[row][slot]))
            for row in range(self.prows)
            for i in range(self.pcols)
        ]


def pick(values, index):
    chosen = jnp.int32(values[0])
    for i, value in enumerate(values[1:], 1):
        chosen = jnp.where(index == i, jnp.int32(value), chosen)
    return chosen


def update_kernel(plan, count, sides, aliased, *refs):
    x_refs, refs = refs[:count], refs[count:]
    strip_refs, refs = refs[: len(sides)], refs[len(sides) :]
    if aliased:
        slab_ref, _, next_ref, column, out_vmem, sems = refs
    else:
        slab_ref, solved_ref, next_ref, factored_ref, column, out_vmem, sems = refs
        factored_copy = pltpu.make_async_copy(solved_ref, factored_ref, sems.at[count])
        factored_copy.start()
    row, me = lax.axis_index("prow"), lax.axis_index("pcol")
    parity = lax.rem(me, 2)
    step = plan.step
    across = pl.ds(0, plan.total)
    if len(sides) == 1:
        across = pl.ds(pl.multiple_of((parity ^ sides[0]) * step, step), step)
        whole = strip_refs[0][...]
    else:
        for s in range(plan.strips_each):
            for ref, side in zip(strip_refs, sides):
                at = pl.multiple_of((2 * s + (parity ^ side)) * step, step)
                column[pl.ds(at, step), :] = ref[s * step : (s + 1) * step, :]
        whole = column[...]
    flips = [pick([f[j] for f in plan.flips], row) for j in range(plan.slots)]
    copies = []
    for n, ref in enumerate(x_refs):
        from_column = me ^ flips[n % plan.slots] ^ (n // plan.slots)
        at = pl.ds(pl.multiple_of(from_column * plan.height, plan.height), plan.height)
        product = lax.dot_general(ref[...], whole, NT, preferred_element_type=jnp.float32)
        out_vmem[at, :] = slab_ref[at, across] - product
        copy = pltpu.make_async_copy(out_vmem.at[at, :], next_ref.at[at, across], sems.at[n])
        copy.start()
        copies.append(copy)
    if not aliased:
        copies.append(factored_copy)
    for copy in copies:
        copy.wait()


def update(plan, solved, strips, sides, slab, own, previous):
    vmem, hbm = pl.BlockSpec(memory_space=pltpu.VMEM), pl.BlockSpec(memory_space=pltpu.HBM)
    aliased = previous is not None
    wide = plan.step * plan.strips_each * len(sides)
    operands = [*solved, *strips, slab, previous if aliased else own]
    outs, out_specs = [jax.ShapeDtypeStruct(slab.shape, jnp.float32)], [hbm]
    if not aliased:
        outs.append(jax.ShapeDtypeStruct(own.shape, jnp.float32))
        out_specs.append(hbm)
    return pl.pallas_call(
        functools.partial(update_kernel, plan, len(solved), sides, aliased),
        out_shape=tuple(outs),
        in_specs=[vmem] * (len(operands) - 1) + [hbm if aliased else vmem],
        out_specs=tuple(out_specs),
        scratch_shapes=[
            pltpu.VMEM((plan.total, own.shape[1]), jnp.bfloat16),
            pltpu.VMEM((slab.shape[0], wide), jnp.float32),
            pltpu.SemaphoreType.DMA((plan.pcols + 1,)),
        ],
        input_output_aliases={len(operands) - 1: 0} if aliased else {},
        cost_estimate=pl.CostEstimate(flops=300_000_000, bytes_accessed=8 * slab.size, transcendentals=0),
        compiler_params=pltpu.CompilerParams(vmem_limit_bytes=8 << 20),
        name="update_rest" if aliased else "update",
    )(*operands)


def choose(options, index):
    chosen = options[0][0]
    for value, indices in options[1:]:
        hit = index == indices[0]
        for i in indices[1:]:
            hit = hit | (index == i)
        chosen = jnp.where(hit, value, chosen)
    return chosen


def per_device(diag_block, panel, slab):
    prows = lax.axis_size("prow")
    pcols = lax.axis_size("pcol")
    width = diag_block.shape[0]
    plan = Plan(prows, pcols, width, panel.shape[0], slab.shape[1] // width)
    row, me = lax.axis_index("prow"), lax.axis_index("pcol")
    device = row * pcols + me
    both = ("prow", "pcol")
    partner = [(i, i ^ 1) for i in range(pcols)]
    opened = mark()
    opened = mark(opened)
    arrived = []
    if plan.slots > 1:
        arrived.append(lax.ppermute(panel, both, plan.pairs(1)))
    inverse, own, low = solve_panel(diag_block, panel, opened, plan.sources, ())
    if plan.far:
        at = plan.far[0][2]
        far = lax.ppermute(low[at : at + plan.step], both, plan.far_pairs())
        inverse, own, low = solve_panel(diag_block, panel, opened, plan.sources, (inverse, own, low))
    for j in range(2, plan.slots):
        arrived.append(lax.ppermute(low, both, plan.pairs(j)))
    solved = [low, *(solve_near(inverse, rows) for rows in arrived[:1]), *arrived[1:]]

    strips = []
    for places in plan.places:
        options = {}
        for at, place in enumerate(places):
            if place is not None:
                options.setdefault(place, []).append(at)
        strips.append(
            choose(
                [(far if j < 0 else solved[j][at : at + plan.step], where) for (j, at), where in options.items()],
                device,
            )
        )
    passed = jnp.concatenate(strips, 0) if len(strips) > 1 else strips[0]
    received = [(passed, [0])]
    for k in range(1, prows):
        received.append((lax.ppermute(passed, "prow", [(i, i ^ k) for i in range(prows)]), [k]))
    for j in range(plan.slots):
        solved.append(lax.ppermute(solved[j], "pcol", partner))
    mine = choose(received, row ^ lax.rem(me, prows))
    other = lax.ppermute(choose(received, row ^ lax.rem(me ^ 1, prows)), "pcol", partner)
    if plan.strips_each == 1 and plan.step % LANES == 0:
        slab_next, factored = update(plan, solved, [mine], (0,), slab, own, None)
        (slab_next,) = update(plan, solved, [other], (1,), slab, own, slab_next)
    else:
        slab_next, factored = update(plan, solved, [mine, other], (0, 1), slab, own, None)
    return slab_next, factored


def solution(mesh):
    placed = (P(), P(("prow", "pcol"), None), P("prow", "pcol"))
    return jax.shard_map(
        per_device,
        mesh=mesh,
        in_specs=placed,
        out_specs=(P("prow", "pcol"), P(("prow", "pcol"), None)),
        check_vma=False,
    )
```

```python
import functools

import jax
import jax.numpy as jnp
from jax import lax
from jax.experimental import pallas as pl
from jax.experimental.pallas import tpu as pltpu
from jax.sharding import PartitionSpec as P


GROUP = 8
LANES = 128
FAR = (-1, 0)
EXACT = lax.Precision.HIGHEST
NT = (((1,), (1,)), ((), ()))


def invert_factor(diag_ref, out_ref):
    n = diag_ref.shape[0]
    groups = n // GROUP
    lane = lax.broadcasted_iota(jnp.int32, (GROUP, n), 1)
    sub = lax.broadcasted_iota(jnp.int32, (GROUP, n), 0)
    rows = [diag_ref[i * GROUP : (i + 1) * GROUP, :] for i in range(groups)]
    zero = jnp.where(lane >= n, rows[0], 0.0)

    def columns(x, first):
        return [jnp.broadcast_to(x[:, at : at + 1], (GROUP, n)) for at in range(first, first + GROUP)]

    def row(x, at):
        return jnp.broadcast_to(x[at : at + 1, :], (GROUP, n))

    cols = [c + zero for c in columns(rows[0], 0)]
    for b in range(groups):
        first = b * GROUP
        inside = (lane >= first) & (lane < first + GROUP)
        work = jnp.where(inside, jnp.where(lane - first == sub, 1.0, 0.0), rows[b])
        scale, scaled, cross = [], [], {}
        follows = b + 1 < groups
        if follows:
            below = columns(rows[b + 1], first)
            ahead = [c + zero for c in columns(rows[b + 1], first + GROUP)]
            rest = jnp.where(inside, 0.0, rows[b + 1])
        for k in range(GROUP):
            scale.append(lax.rsqrt(row(cols[k], k)))
            scaled.append(row(work, k) * scale[k])
            if k < GROUP - 1:
                factor = jnp.where(sub > k, cols[k], 0.0) * scale[k]
                for j in range(k + 1, GROUP):
                    cross[k, j] = row(cols[j], k) * scale[k]
                    cols[j] = cols[j] - factor * cross[k, j]
                work = work - factor * scaled[k]
            if follows:
                factor = below[k] * scale[k]
                for j in range(k + 1, GROUP):
                    below[j] = below[j] - factor * cross[k, j]
                rest = rest - factor * scaled[k]
                for j in range(GROUP):
                    ahead[j] = ahead[j] - factor * row(factor, j)
        done = scaled[0]
        for k in range(1, GROUP):
            done = jnp.where(sub == k, scaled[k], done)
        out_ref[first : first + GROUP, :] = jnp.where(lane <= sub + first, done, 0.0)
        if follows:
            cols = ahead
            rows[b + 1] = rest
        for i in range(b + 2, groups):
            below = columns(rows[i], first)
            rest = jnp.where(inside, 0.0, rows[i])
            for k in range(GROUP):
                factor = below[k] * scale[k]
                for j in range(k + 1, GROUP):
                    below[j] = below[j] - factor * cross[k, j]
                rest = rest - factor * scaled[k]
            rows[i] = rest


def only_for(devices, wanted, body):
    me = lax.axis_index("pcol")
    listed = functools.reduce(jnp.logical_or, [me == i for i in devices])
    pl.when(listed if wanted else jnp.logical_not(listed))(body)


def solve_rows(inverse_ref, rows, solved_ref, low_ref):
    solved = lax.dot_general(rows[...], inverse_ref[...], NT, precision=EXACT, preferred_element_type=jnp.float32)
    low_ref[...] = solved.astype(jnp.bfloat16)
    solved_ref[...] = solved


def panel_kernel(devices, first, panel_hbm, diag_ref, _, *refs):
    inverse, solved_ref, low_ref, panel, sem = refs[-5:]

    def body():
        panel_copy = pltpu.make_async_copy(panel_hbm, panel, sem)
        panel_copy.start()
        invert_factor(diag_ref, inverse)
        panel_copy.wait()
        solve_rows(inverse, panel, solved_ref, low_ref)

    only_for(devices, first, body)


def mark_kernel(*refs):
    refs[-1][...] = jnp.zeros_like(refs[-1])


def mark(*before):
    vmem = pl.BlockSpec(memory_space=pltpu.VMEM)
    return pl.pallas_call(
        mark_kernel,
        out_shape=jax.ShapeDtypeStruct((GROUP, LANES), jnp.float32),
        in_specs=[vmem] * len(before),
        out_specs=vmem,
        cost_estimate=pl.CostEstimate(flops=400_000_000, bytes_accessed=4 * GROUP * LANES, transcendentals=0),
        compiler_params=pltpu.CompilerParams(vmem_limit_bytes=2 << 20),
        name="mark",
    )(*before)


def near_kernel(inverse_ref, rows_ref, low_ref):
    solved = lax.dot_general(
        rows_ref[...], inverse_ref[...], NT, precision=EXACT, preferred_element_type=jnp.float32
    )
    low_ref[...] = solved.astype(jnp.bfloat16)


def solve_near(inverse, rows):
    vmem = pl.BlockSpec(memory_space=pltpu.VMEM)
    return pl.pallas_call(
        near_kernel,
        out_shape=jax.ShapeDtypeStruct(rows.shape, jnp.bfloat16),
        in_specs=[vmem, vmem],
        out_specs=vmem,
        cost_estimate=pl.CostEstimate(flops=200_000_000, bytes_accessed=6 * rows.size, transcendentals=0),
        compiler_params=pltpu.CompilerParams(vmem_limit_bytes=2 << 20),
        name="solve_near",
    )(inverse, rows)


def solve_panel(diag_block, panel, opened, devices, before):
    vmem, hbm = pl.BlockSpec(memory_space=pltpu.VMEM), pl.BlockSpec(memory_space=pl.ANY)
    panel_hbm = pltpu.with_memory_space_constraint(panel, pltpu.HBM)
    return pl.pallas_call(
        functools.partial(panel_kernel, devices, not before),
        out_shape=(
            jax.ShapeDtypeStruct(diag_block.shape, jnp.float32),
            jax.ShapeDtypeStruct(panel.shape, jnp.float32),
            jax.ShapeDtypeStruct(panel.shape, jnp.bfloat16),
        ),
        in_specs=[hbm, vmem, vmem] + [vmem] * len(before),
        out_specs=(vmem, vmem, vmem),
        scratch_shapes=[pltpu.VMEM(panel.shape, jnp.float32), pltpu.SemaphoreType.DMA],
        input_output_aliases={3: 0, 4: 1, 5: 2} if before else {},
        cost_estimate=pl.CostEstimate(flops=2_000_000_000, bytes_accessed=8 * panel.size, transcendentals=0),
        compiler_params=pltpu.CompilerParams(vmem_limit_bytes=2 << 20),
        name="solve_rest" if before else "solve_first",
    )(panel_hbm, diag_block, opened, *before)


class Plan:
    def __init__(self, prows, pcols, width, height, here):
        self.prows, self.pcols, self.height = prows, pcols, height
        self.step = min(width, height)
        spread = pcols // prows

        def strips(column):
            found = []
            for position in range(here):
                block = column // prows + position * spread
                for offset in range(0, width, self.step):
                    at = block * width + offset
                    found.append((at // height, at % height))
            return found

        self.total = here * width
        parity = [shard % 2 for shard, _ in strips(0)]
        assert parity == [s % 2 for s in range(len(parity))]
        self.strips_each = len(parity) // 2
        self.slots = pcols // 2
        self.far = {}
        if self.strips_each == 1:
            for row in range(min(prows, pcols)):
                column = max(range(row, pcols, prows))
                (even, at), (odd, same) = strips(column)
                if at == same and even // 2 == odd // 2 != column // 2:
                    self.far[row] = (column, even // 2, at)
        if len(self.far) < prows or len({at for _, _, at in self.far.values()}) > 1:
            self.far = {}
        self.sources = sorted({2 * chip + t for _, chip, _ in self.far.values() for t in range(2)})
        if not self.far:
            self.sources = range(pcols)
        self.flips = []
        for row in range(prows):
            first = []
            for column in range(row, pcols, prows):
                if self.far and column == self.far[row][0]:
                    continue
                for shard, _ in strips(column):
                    k = 2 * ((shard // 2) ^ (column // 2))
                    if k and k not in first:
                        first.append(k)
            first.sort(reverse=True)
            rest = [k for k in range(pcols - 2, 0, -2) if k not in first]
            self.flips.append([0] + sorted(first + rest, key=lambda k: (k != 2, k)))
        self.places = [[None] * (prows * pcols) for _ in range(self.strips_each)]
        for row in range(prows):
            for me in range(pcols):
                for column in (me, me ^ 1):
                    if column % prows == row:
                        if self.far and column == self.far[row][0]:
                            self.places[0][row * pcols + me] = FAR
                            continue
                        own = [s for s in strips(column) if s[0] % 2 == me % 2]
                        for n, (shard, at) in enumerate(own):
                            slot = self.flips[row].index(2 * ((shard // 2) ^ (me // 2)))
                            self.places[n][row * pcols + me] = (slot, at)

    def far_pairs(self):
        return [
            (row * self.pcols + 2 * chip + t, row * self.pcols + (column // 2) * 2 + t)
            for row, (column, chip, _) in self.far.items()
            for t in range(2)
        ]

    def pairs(self, slot):
        return [
            (row * self.pcols + i, row * self.pcols + (i ^ self.flips[row][slot]))
            for row in range(self.prows)
            for i in range(self.pcols)
        ]


def pick(values, index):
    chosen = jnp.int32(values[0])
    for i, value in enumerate(values[1:], 1):
        chosen = jnp.where(index == i, jnp.int32(value), chosen)
    return chosen


def update_kernel(plan, slots, sides, jobs, aliased, *refs):
    x_refs, refs = refs[: len(slots)], refs[len(slots) :]
    strip_refs, refs = refs[: len(sides)], refs[len(sides) :]
    copies = []
    if aliased:
        slab_ref, _, next_ref, column, out_vmem, sems = refs
    else:
        slab_ref, solved_ref, next_ref, factored_ref, column, out_vmem, sems = refs
        copies.append(pltpu.make_async_copy(solved_ref, factored_ref, sems.at[0]))
        copies[0].start()
    row, me = lax.axis_index("prow"), lax.axis_index("pcol")
    parity = lax.rem(me, 2)
    step = plan.step
    if jobs is None:
        for s in range(plan.strips_each):
            for ref, side in zip(strip_refs, sides):
                at = pl.multiple_of((2 * s + (parity ^ side)) * step, step)
                column[pl.ds(at, step), :] = ref[s * step : (s + 1) * step, :]
        parts = [(i, column[...], pl.ds(0, plan.total), pl.ds(0, plan.total)) for i in range(len(slots))]
    else:
        parts = [
            (
                i,
                strip_refs[c][...],
                pl.ds(pl.multiple_of((parity ^ sides[c]) * step, step), step),
                pl.ds(c * step, step),
            )
            for i, c in jobs
        ]
    flips = [pick([f[j] for f in plan.flips], row) for j in range(plan.slots)]
    for n, (i, strip, across, held) in enumerate(parts):
        slot, side = slots[i]
        at = pl.ds(pl.multiple_of((me ^ flips[slot] ^ side) * plan.height, plan.height), plan.height)
        product = lax.dot_general(x_refs[i][...], strip, NT, preferred_element_type=jnp.float32)
        out_vmem[at, held] = slab_ref[at, across] - product
        copy = pltpu.make_async_copy(out_vmem.at[at, held], next_ref.at[at, across], sems.at[n + 1])
        copy.start()
        copies.append(copy)
    for copy in copies:
        copy.wait()


def update(plan, solved, slots, strips, sides, jobs, slab, own, previous):
    vmem, hbm = pl.BlockSpec(memory_space=pltpu.VMEM), pl.BlockSpec(memory_space=pltpu.HBM)
    aliased = previous is not None
    wide = plan.step * plan.strips_each * len(sides)
    operands = [*solved, *strips, slab, previous if aliased else own]
    outs, out_specs = [jax.ShapeDtypeStruct(slab.shape, jnp.float32)], [hbm]
    if not aliased:
        outs.append(jax.ShapeDtypeStruct(own.shape, jnp.float32))
        out_specs.append(hbm)
    return pl.pallas_call(
        functools.partial(update_kernel, plan, slots, sides, jobs, aliased),
        out_shape=tuple(outs),
        in_specs=[vmem] * (len(operands) - 1) + [hbm if aliased else vmem],
        out_specs=tuple(out_specs),
        scratch_shapes=[
            pltpu.VMEM((plan.total, own.shape[1]), jnp.bfloat16),
            pltpu.VMEM((slab.shape[0], wide), jnp.float32),
            pltpu.SemaphoreType.DMA((len(jobs or solved) + 1,)),
        ],
        input_output_aliases={len(operands) - 1: 0} if aliased else {},
        cost_estimate=pl.CostEstimate(flops=300_000_000, bytes_accessed=8 * slab.size, transcendentals=0),
        compiler_params=pltpu.CompilerParams(vmem_limit_bytes=8 << 20),
        name="update_rest" if aliased else "update",
    )(*operands)


def choose(options, index):
    chosen = options[0][0]
    for value, indices in options[1:]:
        hit = index == indices[0]
        for i in indices[1:]:
            hit = hit | (index == i)
        chosen = jnp.where(hit, value, chosen)
    return chosen


def per_device(diag_block, panel, slab):
    prows = lax.axis_size("prow")
    pcols = lax.axis_size("pcol")
    width = diag_block.shape[0]
    plan = Plan(prows, pcols, width, panel.shape[0], slab.shape[1] // width)
    row, me = lax.axis_index("prow"), lax.axis_index("pcol")
    device = row * pcols + me
    both = ("prow", "pcol")
    partner = [(i, i ^ 1) for i in range(pcols)]
    opened = mark()
    opened = mark(opened)
    arrived = []
    if plan.slots > 1:
        arrived.append(lax.ppermute(panel, both, plan.pairs(1)))
    inverse, own, low = solve_panel(diag_block, panel, opened, plan.sources, ())
    if plan.far:
        at = plan.far[0][2]
        far = lax.ppermute(low[at : at + plan.step], both, plan.far_pairs())
        inverse, own, low = solve_panel(diag_block, panel, opened, plan.sources, (inverse, own, low))
    for j in range(2, plan.slots):
        arrived.append(lax.ppermute(low, both, plan.pairs(j)))
    solved = [low, *(solve_near(inverse, rows) for rows in arrived[:1]), *arrived[1:]]

    strips = []
    for places in plan.places:
        options = {}
        for at, place in enumerate(places):
            if place is not None:
                options.setdefault(place, []).append(at)
        strips.append(
            choose(
                [(far if j < 0 else solved[j][at : at + plan.step], where) for (j, at), where in options.items()],
                device,
            )
        )
    passed = jnp.concatenate(strips, 0) if len(strips) > 1 else strips[0]
    received = [(passed, [0])]
    for k in range(1, prows):
        received.append((lax.ppermute(passed, "prow", [(i, i ^ k) for i in range(prows)]), [k]))
    for j in range(plan.slots):
        solved.append(lax.ppermute(solved[j], "pcol", partner))
    mine = choose(received, row ^ lax.rem(me, prows))
    other = lax.ppermute(choose(received, row ^ lax.rem(me ^ 1, prows)), "pcol", partner)
    slots = [(n % plan.slots, n // plan.slots) for n in range(len(solved))]
    if plan.strips_each == 1 and plan.step % LANES == 0:
        last = len(solved) - 1
        slab_next, factored = update(
            plan, solved[:last], slots[:last], [mine], (0,), [(i, 0) for i in range(last)], slab, own, None
        )
        jobs = [(i, 0) for i in range(last + 1)] + [(last, 1)]
        (slab_next,) = update(plan, solved, slots, [other, mine], (1, 0), jobs, slab, own, slab_next)
    else:
        slab_next, factored = update(plan, solved, slots, [mine, other], (0, 1), None, slab, own, None)
    return slab_next, factored


def solution(mesh):
    placed = (P(), P(("prow", "pcol"), None), P("prow", "pcol"))
    return jax.shard_map(
        per_device,
        mesh=mesh,
        in_specs=placed,
        out_specs=(P("prow", "pcol"), P(("prow", "pcol"), None)),
        check_vma=False,
    )
```

```python
import functools

import jax
import jax.numpy as jnp
from jax import lax
from jax.experimental import pallas as pl
from jax.experimental.pallas import tpu as pltpu
from jax.sharding import PartitionSpec as P


GROUP = 8
LANES = 128
FAR = (-1, 0)
EXACT = lax.Precision.HIGHEST
NT = (((1,), (1,)), ((), ()))


def invert_factor(diag_ref, out_ref):
    n = diag_ref.shape[0]
    groups = n // GROUP
    lane = lax.broadcasted_iota(jnp.int32, (GROUP, n), 1)
    sub = lax.broadcasted_iota(jnp.int32, (GROUP, n), 0)
    rows = [diag_ref[i * GROUP : (i + 1) * GROUP, :] for i in range(groups)]
    zero = jnp.where(lane >= n, rows[0], 0.0)

    def columns(x, first):
        return [jnp.broadcast_to(x[:, at : at + 1], (GROUP, n)) for at in range(first, first + GROUP)]

    def row(x, at):
        return jnp.broadcast_to(x[at : at + 1, :], (GROUP, n))

    cols = [c + zero for c in columns(rows[0], 0)]
    for b in range(groups):
        first = b * GROUP
        inside = (lane >= first) & (lane < first + GROUP)
        work = jnp.where(inside, jnp.where(lane - first == sub, 1.0, 0.0), rows[b])
        scale, scaled, cross = [], [], {}
        follows = b + 1 < groups
        if follows:
            below = columns(rows[b + 1], first)
            ahead = [c + zero for c in columns(rows[b + 1], first + GROUP)]
            rest = jnp.where(inside, 0.0, rows[b + 1])
        for k in range(GROUP):
            scale.append(lax.rsqrt(row(cols[k], k)))
            scaled.append(row(work, k) * scale[k])
            if k < GROUP - 1:
                factor = jnp.where(sub > k, cols[k], 0.0) * scale[k]
                for j in range(k + 1, GROUP):
                    cross[k, j] = row(cols[j], k) * scale[k]
                    cols[j] = cols[j] - factor * cross[k, j]
                work = work - factor * scaled[k]
            if follows:
                factor = below[k] * scale[k]
                for j in range(k + 1, GROUP):
                    below[j] = below[j] - factor * cross[k, j]
                rest = rest - factor * scaled[k]
                for j in range(GROUP):
                    ahead[j] = ahead[j] - factor * row(factor, j)
        done = scaled[0]
        for k in range(1, GROUP):
            done = jnp.where(sub == k, scaled[k], done)
        out_ref[first : first + GROUP, :] = jnp.where(lane <= sub + first, done, 0.0)
        if follows:
            cols = ahead
            rows[b + 1] = rest
        for i in range(b + 2, groups):
            below = columns(rows[i], first)
            rest = jnp.where(inside, 0.0, rows[i])
            for k in range(GROUP):
                factor = below[k] * scale[k]
                for j in range(k + 1, GROUP):
                    below[j] = below[j] - factor * cross[k, j]
                rest = rest - factor * scaled[k]
            rows[i] = rest


def only_for(devices, wanted, body):
    me = lax.axis_index("pcol")
    listed = functools.reduce(jnp.logical_or, [me == i for i in devices])
    pl.when(listed if wanted else jnp.logical_not(listed))(body)


def solve_rows(inverse_ref, rows, solved_ref, low_ref):
    solved = lax.dot_general(rows[...], inverse_ref[...], NT, precision=EXACT, preferred_element_type=jnp.float32)
    low_ref[...] = solved.astype(jnp.bfloat16)
    solved_ref[...] = solved


def panel_kernel(devices, first, panel_hbm, diag_ref, _, *refs):
    inverse, solved_ref, low_ref, panel, sem = refs[-5:]

    def body():
        panel_copy = pltpu.make_async_copy(panel_hbm, panel, sem)
        panel_copy.start()
        invert_factor(diag_ref, inverse)
        panel_copy.wait()
        solve_rows(inverse, panel, solved_ref, low_ref)

    only_for(devices, first, body)


def mark_kernel(*refs):
    refs[-1][...] = jnp.zeros_like(refs[-1])


def mark(*before):
    vmem = pl.BlockSpec(memory_space=pltpu.VMEM)
    return pl.pallas_call(
        mark_kernel,
        out_shape=jax.ShapeDtypeStruct((GROUP, LANES), jnp.float32),
        in_specs=[vmem] * len(before),
        out_specs=vmem,
        cost_estimate=pl.CostEstimate(flops=400_000_000, bytes_accessed=4 * GROUP * LANES, transcendentals=0),
        compiler_params=pltpu.CompilerParams(vmem_limit_bytes=2 << 20),
        name="mark",
    )(*before)


def near_kernel(first, inverse_ref, rows_ref, low_ref):
    rows = rows_ref[first : first + low_ref.shape[0], :]
    solved = lax.dot_general(rows, inverse_ref[...], NT, precision=EXACT, preferred_element_type=jnp.float32)
    low_ref[...] = solved.astype(jnp.bfloat16)


def solve_near(inverse, rows, first, count):
    vmem = pl.BlockSpec(memory_space=pltpu.VMEM)
    return pl.pallas_call(
        functools.partial(near_kernel, first),
        out_shape=jax.ShapeDtypeStruct((count, rows.shape[1]), jnp.bfloat16),
        in_specs=[vmem, vmem],
        out_specs=vmem,
        cost_estimate=pl.CostEstimate(flops=200_000_000, bytes_accessed=6 * rows.size, transcendentals=0),
        compiler_params=pltpu.CompilerParams(vmem_limit_bytes=2 << 20),
        name="solve_near",
    )(inverse, rows)


def solve_panel(diag_block, panel, opened, devices, before):
    vmem, hbm = pl.BlockSpec(memory_space=pltpu.VMEM), pl.BlockSpec(memory_space=pl.ANY)
    panel_hbm = pltpu.with_memory_space_constraint(panel, pltpu.HBM)
    return pl.pallas_call(
        functools.partial(panel_kernel, devices, not before),
        out_shape=(
            jax.ShapeDtypeStruct(diag_block.shape, jnp.float32),
            jax.ShapeDtypeStruct(panel.shape, jnp.float32),
            jax.ShapeDtypeStruct(panel.shape, jnp.bfloat16),
        ),
        in_specs=[hbm, vmem, vmem] + [vmem] * len(before),
        out_specs=(vmem, vmem, vmem),
        scratch_shapes=[pltpu.VMEM(panel.shape, jnp.float32), pltpu.SemaphoreType.DMA],
        input_output_aliases={3: 0, 4: 1, 5: 2} if before else {},
        cost_estimate=pl.CostEstimate(flops=2_000_000_000, bytes_accessed=8 * panel.size, transcendentals=0),
        compiler_params=pltpu.CompilerParams(vmem_limit_bytes=2 << 20),
        name="solve_rest" if before else "solve_first",
    )(panel_hbm, diag_block, opened, *before)


class Plan:
    def __init__(self, prows, pcols, width, height, here):
        self.prows, self.pcols, self.height = prows, pcols, height
        self.step = min(width, height)
        spread = pcols // prows

        def strips(column):
            found = []
            for position in range(here):
                block = column // prows + position * spread
                for offset in range(0, width, self.step):
                    at = block * width + offset
                    found.append((at // height, at % height))
            return found

        self.total = here * width
        parity = [shard % 2 for shard, _ in strips(0)]
        assert parity == [s % 2 for s in range(len(parity))]
        self.strips_each = len(parity) // 2
        self.slots = pcols // 2
        self.far = {}
        if self.strips_each == 1:
            for row in range(min(prows, pcols)):
                column = max(range(row, pcols, prows))
                (even, at), (odd, same) = strips(column)
                if at == same and even // 2 == odd // 2 != column // 2:
                    self.far[row] = (column, even // 2, at)
        if len(self.far) < prows or len({at for _, _, at in self.far.values()}) > 1:
            self.far = {}
        self.sources = sorted({2 * chip + t for _, chip, _ in self.far.values() for t in range(2)})
        if not self.far:
            self.sources = range(pcols)
        self.flips = []
        for row in range(prows):
            first = []
            for column in range(row, pcols, prows):
                if self.far and column == self.far[row][0]:
                    continue
                for shard, _ in strips(column):
                    k = 2 * ((shard // 2) ^ (column // 2))
                    if k and k not in first:
                        first.append(k)
            first.sort(reverse=True)
            rest = [k for k in range(pcols - 2, 0, -2) if k not in first]
            self.flips.append([0] + sorted(first + rest, key=lambda k: (k != 2, k)))
        self.places = [[None] * (prows * pcols) for _ in range(self.strips_each)]
        for row in range(prows):
            for me in range(pcols):
                for column in (me, me ^ 1):
                    if column % prows == row:
                        if self.far and column == self.far[row][0]:
                            self.places[0][row * pcols + me] = FAR
                            continue
                        own = [s for s in strips(column) if s[0] % 2 == me % 2]
                        for n, (shard, at) in enumerate(own):
                            slot = self.flips[row].index(2 * ((shard // 2) ^ (me // 2)))
                            self.places[n][row * pcols + me] = (slot, at)

    def far_pairs(self):
        return [
            (row * self.pcols + 2 * chip + t, row * self.pcols + (column // 2) * 2 + t)
            for row, (column, chip, _) in self.far.items()
            for t in range(2)
        ]

    def pairs(self, slot):
        return [
            (row * self.pcols + i, row * self.pcols + (i ^ self.flips[row][slot]))
            for row in range(self.prows)
            for i in range(self.pcols)
        ]


def pick(values, index):
    chosen = jnp.int32(values[0])
    for i, value in enumerate(values[1:], 1):
        chosen = jnp.where(index == i, jnp.int32(value), chosen)
    return chosen


def update_kernel(plan, slots, sides, jobs, aliased, *refs):
    x_refs, refs = refs[: len(slots)], refs[len(slots) :]
    strip_refs, refs = refs[: len(sides)], refs[len(sides) :]
    copies = []
    if aliased:
        slab_ref, _, next_ref, column, out_vmem, sems = refs
    else:
        slab_ref, solved_ref, next_ref, factored_ref, column, out_vmem, sems = refs
        copies.append(pltpu.make_async_copy(solved_ref, factored_ref, sems.at[0]))
        copies[0].start()
    row, me = lax.axis_index("prow"), lax.axis_index("pcol")
    parity = lax.rem(me, 2)
    step = plan.step
    if jobs is None:
        for s in range(plan.strips_each):
            for ref, side in zip(strip_refs, sides):
                at = pl.multiple_of((2 * s + (parity ^ side)) * step, step)
                column[pl.ds(at, step), :] = ref[s * step : (s + 1) * step, :]
        parts = [(i, column[...], pl.ds(0, plan.total), pl.ds(0, plan.total)) for i in range(len(slots))]
    else:
        parts = [
            (
                i,
                strip_refs[c][...],
                pl.ds(pl.multiple_of((parity ^ sides[c]) * step, step), step),
                pl.ds(c * step, step),
            )
            for i, c in jobs
        ]
    flips = [pick([f[j] for f in plan.flips], row) for j in range(plan.slots)]
    for n, (i, strip, across, held) in enumerate(parts):
        slot, side = slots[i]
        at = pl.ds(pl.multiple_of((me ^ flips[slot] ^ side) * plan.height, plan.height), plan.height)
        product = lax.dot_general(x_refs[i][...], strip, NT, preferred_element_type=jnp.float32)
        out_vmem[at, held] = slab_ref[at, across] - product
        copy = pltpu.make_async_copy(out_vmem.at[at, held], next_ref.at[at, across], sems.at[n + 1])
        copy.start()
        copies.append(copy)
    for copy in copies:
        copy.wait()


def update(plan, solved, slots, strips, sides, jobs, slab, own, previous):
    vmem, hbm = pl.BlockSpec(memory_space=pltpu.VMEM), pl.BlockSpec(memory_space=pltpu.HBM)
    aliased = previous is not None
    wide = plan.step * plan.strips_each * len(sides)
    operands = [*solved, *strips, slab, previous if aliased else own]
    outs, out_specs = [jax.ShapeDtypeStruct(slab.shape, jnp.float32)], [hbm]
    if not aliased:
        outs.append(jax.ShapeDtypeStruct(own.shape, jnp.float32))
        out_specs.append(hbm)
    return pl.pallas_call(
        functools.partial(update_kernel, plan, slots, sides, jobs, aliased),
        out_shape=tuple(outs),
        in_specs=[vmem] * (len(operands) - 1) + [hbm if aliased else vmem],
        out_specs=tuple(out_specs),
        scratch_shapes=[
            pltpu.VMEM((plan.total, own.shape[1]), jnp.bfloat16),
            pltpu.VMEM((slab.shape[0], wide), jnp.float32),
            pltpu.SemaphoreType.DMA((len(jobs or solved) + 1,)),
        ],
        input_output_aliases={len(operands) - 1: 0} if aliased else {},
        cost_estimate=pl.CostEstimate(flops=300_000_000, bytes_accessed=8 * slab.size, transcendentals=0),
        compiler_params=pltpu.CompilerParams(vmem_limit_bytes=8 << 20),
        name="update_rest" if aliased else "update",
    )(*operands)


def choose(options, index):
    chosen = options[0][0]
    for value, indices in options[1:]:
        hit = index == indices[0]
        for i in indices[1:]:
            hit = hit | (index == i)
        chosen = jnp.where(hit, value, chosen)
    return chosen


def per_device(diag_block, panel, slab):
    prows = lax.axis_size("prow")
    pcols = lax.axis_size("pcol")
    width = diag_block.shape[0]
    plan = Plan(prows, pcols, width, panel.shape[0], slab.shape[1] // width)
    row, me = lax.axis_index("prow"), lax.axis_index("pcol")
    device = row * pcols + me
    both = ("prow", "pcol")
    partner = [(i, i ^ 1) for i in range(pcols)]
    opened = mark()
    opened = mark(opened)
    arrived = []
    if plan.slots > 1:
        arrived.append(lax.ppermute(panel, both, plan.pairs(1)))
    inverse, own, low = solve_panel(diag_block, panel, opened, plan.sources, ())
    if plan.far:
        at = plan.far[0][2]
        far = lax.ppermute(low[at : at + plan.step], both, plan.far_pairs())
        inverse, own, low = solve_panel(diag_block, panel, opened, plan.sources, (inverse, own, low))
    for j in range(2, plan.slots):
        arrived.append(lax.ppermute(low, both, plan.pairs(j)))
    solved = [low, *(solve_near(inverse, rows, 0, plan.height) for rows in arrived[:1]), *arrived[1:]]

    def strip_at(slot, at):
        if slot < 0:
            return far
        if slot == 1:
            return solve_near(inverse, arrived[0], at, plan.step)
        return solved[slot][at : at + plan.step]

    strips = []
    for places in plan.places:
        options = {}
        for at, place in enumerate(places):
            if place is not None:
                options.setdefault(place, []).append(at)
        strips.append(
            choose(
                [(strip_at(j, at), where) for (j, at), where in options.items()],
                device,
            )
        )
    passed = jnp.concatenate(strips, 0) if len(strips) > 1 else strips[0]
    received = [(passed, [0])]
    for k in range(1, prows):
        received.append((lax.ppermute(passed, "prow", [(i, i ^ k) for i in range(prows)]), [k]))
    for j in range(plan.slots):
        solved.append(lax.ppermute(solved[j], "pcol", partner))
    mine = choose(received, row ^ lax.rem(me, prows))
    other = lax.ppermute(choose(received, row ^ lax.rem(me ^ 1, prows)), "pcol", partner)
    slots = [(n % plan.slots, n // plan.slots) for n in range(len(solved))]
    if plan.strips_each == 1 and plan.step % LANES == 0:
        last = len(solved) - 1
        slab_next, factored = update(
            plan, solved[:last], slots[:last], [mine], (0,), [(i, 0) for i in range(last)], slab, own, None
        )
        jobs = [(last, 1), (last, 0)] + [(i, 0) for i in range(last)]
        (slab_next,) = update(plan, solved, slots, [other, mine], (1, 0), jobs, slab, own, slab_next)
    else:
        slab_next, factored = update(plan, solved, slots, [mine, other], (0, 1), None, slab, own, None)
    return slab_next, factored


def solution(mesh):
    placed = (P(), P(("prow", "pcol"), None), P("prow", "pcol"))
    return jax.shard_map(
        per_device,
        mesh=mesh,
        in_specs=placed,
        out_specs=(P("prow", "pcol"), P(("prow", "pcol"), None)),
        check_vma=False,
    )
```
